256 devices in a mesh: node: 64 (over z, y, core), samp: 4 (over x).
Axes of the slice: x: 4, y: 4, z: 8, core: 2. Of those that a mesh axis runs over, the one named last changes fastest.
Arguments:
- snapshots: bfloat16 [524288, 2048], P('node', 'samp'), may hold values from -330 to 330
- sketch_matrix: bfloat16 [2048, 160], P('samp'), may hold values from -0.125 to 0.125
Outputs:
- core_rows: float32 [524288, 160], P(('node', 'samp'))
- next_rows: float32 [10240, 32], P('node', 'samp')
The draws below stay inside these ranges and needn't reach their ends.
All inputs are finite; a program needn't handle non-finite values.
Results may differ from the reference program's by a relative error of at most 0.00045.
Values may be sent and summed in bfloat16 or wider, within the bound.
A program may use at most 64 MiB of HBM per device.

```python
import math
import jax
import jax.numpy as jnp
from jax import lax

ROWS_DEV = 8192
R = 160
P1 = 64
P2 = 32
NODES = 524288
SAMPLES = 2048
N_NODE = 64


def draw_snapshots(key, part):
    key_noise, key_rows, key_cols, key_mode_rows, key_mode_cols = jax.random.split(key, 5)
    position = jnp.arange(NODES, dtype=jnp.float32) / NODES
    noise_part = jax.random.truncated_normal(key_noise, -4.0, 4.0, (NODES, SAMPLES), jnp.float32)
    row_spread = math.log(10.0)
    common = 0.8
    row_scale = jnp.exp(jax.random.uniform(key_rows, (NODES,), jnp.float32, 0.0, row_spread)) * (1.0 + 2.0 * position)
    col_scale = jnp.exp(jax.random.uniform(key_cols, (SAMPLES,), jnp.float32, 0.0, math.log(10.0)))
    mode_rows = jax.random.truncated_normal(key_mode_rows, -3.0, 3.0, (NODES,), jnp.float32)
    mode_cols = jax.random.truncated_normal(key_mode_cols, -3.0, 3.0, (SAMPLES,), jnp.float32)
    values = row_scale[:, None] * col_scale[None, :] * (noise_part + common * mode_rows[:, None] * mode_cols[None, :])
    return (0.05 * values).astype(jnp.bfloat16)


def levels(key, extent, shards, low, top_value):
    loudness = 1.0
    for dim, shards_of in shards:
        heights = jax.random.uniform(jax.random.fold_in(jax.random.fold_in(key, 6), dim), (shards_of,), jnp.float32, low / len(shards), top_value / len(shards))
        loudness = loudness * jnp.repeat(jnp.exp(heights), extent[dim] // shards_of).reshape((-1,) + (1,) * (len(extent) - 1 - dim))
    return loudness


def gaussian(rng, extent, deviation, bound, shards=(), kind=jnp.bfloat16):
    array = deviation * jax.random.normal(rng, extent, jnp.float32)
    if shards:
        array = array * levels(rng, extent, shards, -0.22, 0.18)
    return jnp.clip(array, -bound, bound).astype(kind)


def setup_inputs(seed: int = 0) -> dict:
    key_of = jax.random.split(jax.random.key(seed), 3)
    return {
        "snapshots": draw_snapshots(jax.random.fold_in(key_of[2], 71), 0),
        "sketch_matrix": gaussian(key_of[1], (SAMPLES, R), (P1 * P2) ** -0.5, 0.125, ((0, 4),)),
    }


def reference(snapshots, sketch_matrix):
    row_blocks = snapshots.reshape(N_NODE, ROWS_DEV, P1 * P2)

    def sketch_block(row_block):
        return jnp.dot(row_block.astype(jnp.float32), sketch_matrix.astype(jnp.float32), preferred_element_type=jnp.float32)
    sketched = lax.map(sketch_block, row_blocks).reshape(NODES, R)
    gram_matrix = jnp.dot(sketched.T.astype(jnp.float32), sketched.astype(jnp.float32), precision=lax.Precision.HIGHEST, preferred_element_type=jnp.float32) / NODES
    factor_lower = jnp.linalg.cholesky(gram_matrix)
    identity = jnp.eye(R, dtype=jnp.float32)
    inverse = lax.linalg.triangular_solve(factor_lower, identity, left_side=True, lower=True)
    core_rows = jnp.dot(sketched.astype(jnp.float32), inverse.T.astype(jnp.float32), precision=lax.Precision.HIGHEST, preferred_element_type=jnp.float32)
    basis_rows = core_rows.astype(jnp.bfloat16).reshape(N_NODE, ROWS_DEV, R)

    def project_block(paired):
        return jnp.dot(paired[0].T.astype(jnp.float32), paired[1].astype(jnp.float32), preferred_element_type=jnp.float32)
    partial_sums = lax.map(project_block, (basis_rows, row_blocks))
    coefficients = jnp.sum(partial_sums, axis=0) / NODES
    next_rows = coefficients.reshape(R, P1, P2).transpose(1, 0, 2).reshape(P1 * R, P2)
    return (core_rows, next_rows)
```

```python
import functools
import jax
import jax.numpy as jnp
from jax import lax
from jax.experimental import pallas as pl
from jax.experimental.pallas import tpu as pltpu
from jax.sharding import PartitionSpec as P

MESH = pl.DeviceIdType.MESH
HIGH = lax.Precision.HIGHEST
R = 160
PC = 512
NT = (((1,), (1,)), ((), ()))
F32 = jnp.float32
BF16 = jnp.bfloat16
PANEL = 32


def sketch_kernel(s_hbm, om_ref, y_ref, gp_ref, ct_ref,
                  sv, sl, sr, rl, rr, yown, yr, yl, yopp, cacc, gacc,
                  load_sem, sls, srs, rls, rrs, gsl, gsr, grr, grl, fsl, fsr, frr, frl):
    me = lax.axis_index("samp")
    left = lax.rem(me + 3, 4)
    right = lax.rem(me + 1, 4)
    opp = lax.rem(me + 2, 4)

    barrier = pltpu.get_barrier_semaphore()
    for peer in (left, right):
        pl.semaphore_signal(barrier, inc=1, device_id={"samp": peer}, device_id_type=MESH)

    order = [(opp, 0), (opp, 2), (opp, 1), (opp, 3),
             (left, 2), (right, 0), (left, 3), (right, 1),
             (left, 0), (right, 2), (left, 1), (right, 3),
             (me, 0), (me, 2), (me, 1), (me, 3)]
    where = {"opp": [0, 2, 1, 3], "left": [8, 10, 4, 6], "right": [5, 7, 9, 11], "me": [12, 14, 13, 15]}

    loads = []
    for pos, (chunk, piece) in enumerate(order):
        start = pl.multiple_of(chunk * 2048 + piece * PC, PC)
        copy = pltpu.make_async_copy(s_hbm.at[pl.ds(start, PC), :], sv.at[pos], load_sem.at[pos])
        copy.start()
        loads.append(copy)

    def sketch(pos):
        loads[pos].wait()
        return lax.dot_general(om_ref[...], sv[pos], NT, preferred_element_type=F32)

    def send(src, dst, ssem, rsem, peer):
        copy = pltpu.make_async_remote_copy(src_ref=src, dst_ref=dst, send_sem=ssem, recv_sem=rsem,
                                            device_id={"samp": peer}, device_id_type=MESH)
        copy.start()
        return copy

    to_left = [None] * 6
    to_right = [None] * 6

    def send_left(k):
        to_left[k] = send(sl.at[k], rr.at[k], sls.at[k], rrs.at[k], left)

    def send_right(k):
        to_right[k] = send(sr.at[k], rl.at[k], srs.at[k], rls.at[k], right)

    sl[0] = sketch(0)
    sr[0] = sketch(1)
    pl.semaphore_wait(barrier, 2)
    send_left(0)
    send_right(0)
    for k, (a, b) in enumerate([(2, 3), (4, 5), (6, 7)]):
        sl[k + 1] = sketch(a)
        send_left(k + 1)
        sr[k + 1] = sketch(b)
        send_right(k + 1)
    sl[4] = sketch(8)
    sr[4] = sketch(9)
    sl[5] = sketch(10)
    sr[5] = sketch(11)
    for pos, piece in ((12, 0), (13, 2), (14, 1), (15, 3)):
        y_ref[:, piece * PC:(piece + 1) * PC] = sketch(pos)

    for k in range(2):
        to_left[k].wait_recv()
        sl[4 + k] = sl[4 + k] + rr[k]
        send_left(4 + k)
        to_right[k].wait_recv()
        sr[4 + k] = sr[4 + k] + rl[k]
        send_right(4 + k)

    for k in range(2):
        to_right[2 + k].wait_recv()
        y_ref[:, k * PC:(k + 1) * PC] += rl[2 + k]
        to_left[2 + k].wait_recv()
        y_ref[:, (2 + k) * PC:(3 + k) * PC] += rr[2 + k]

    gather_left = [None] * 4
    gather_right = [None] * 4

    def finish(piece, last, first):
        columns = slice(piece * PC, (piece + 1) * PC)
        value = y_ref[:, columns] + last
        y_ref[:, columns] = value
        rounded = value.astype(BF16)
        yown[piece] = rounded
        gather_left[piece] = send(yown.at[piece], yr.at[piece], gsl.at[piece], grr.at[piece], left)
        gather_right[piece] = send(yown.at[piece], yl.at[piece], gsr.at[piece], grl.at[piece], right)
        gram = lax.dot_general(value, value, NT, precision=HIGH, preferred_element_type=F32)
        coeff = jnp.dot(rounded, sv[where["me"][piece]], preferred_element_type=F32)
        if first:
            gacc[...] = gram
            cacc[...] = coeff
        else:
            gacc[...] += gram
            cacc[...] += coeff

    to_left[4].wait_recv()
    finish(0, rr[4], True)
    to_right[4].wait_recv()
    finish(2, rl[4], False)
    to_left[5].wait_recv()
    finish(1, rr[5], False)
    to_right[5].wait_recv()
    finish(3, rl[5], False)

    gram = gacc[...]
    gp_ref[0:20] = gram[:, 0:128].reshape(20, 8, 128)
    gp_ref[20:32] = jnp.zeros((12, 8, 128), F32)
    gp_ref[20:24, :, 0:32] = gram[128:160, 128:160].reshape(4, 8, 32)

    forward = [None] * 4
    for piece in (0, 2, 1, 3):
        gather_left[piece].wait_recv()
        if piece in (0, 2):
            forward[piece] = send(yr.at[piece], yopp.at[piece], fsl.at[piece // 2], frr.at[piece // 2], left)
        gather_right[piece].wait_recv()
        if piece in (1, 3):
            forward[piece] = send(yl.at[piece], yopp.at[piece], fsr.at[piece // 2], frl.at[piece // 2], right)
        cacc[...] += jnp.dot(yr[piece], sv[where["right"][piece]], preferred_element_type=F32)
        cacc[...] += jnp.dot(yl[piece], sv[where["left"][piece]], preferred_element_type=F32)
    for piece in (0, 2, 1, 3):
        forward[piece].wait_recv()
        cacc[...] += jnp.dot(yopp[piece], sv[where["opp"][piece]], preferred_element_type=F32)

    turned = cacc[...].T
    for zl in range(2):
        for v in range(8):
            ct_ref[v, zl * 32:(zl + 1) * 32, :] = turned[(zl * 8 + v) * 32:(zl * 8 + v + 1) * 32, :]

    for copy in to_left + to_right + gather_left + gather_right + forward:
        copy.wait_send()


def reduce_kernel(gp_ref, ct_ref, gfull_ref, cred_ref, gin, part, zin, cin, csum, cz,
                  gss, grs, zss, zrs, ass, ars, css, crs, dss, drs):
    node = lax.axis_index("node")
    x = lax.axis_index("samp")
    z = node // 8
    v = lax.rem(node, 8)
    u = x * 8 + v

    barrier = pltpu.get_barrier_semaphore()

    def ids(node_to, samp_to):
        return {"node": node_to, "samp": samp_to}

    def group_peer(i):
        w = lax.rem(u + i, 32)
        return w, ids(z * 8 + lax.rem(w, 8), w // 8)

    def z_peer(i):
        w = lax.rem(z + i, 8)
        return w, ids(w * 8 + v, x)

    def greet(i, carry):
        pl.semaphore_signal(barrier, inc=1, device_id=group_peer(i)[1], device_id_type=MESH)
        return carry

    lax.fori_loop(1, 32, greet, 0)
    for i in range(1, 8):
        pl.semaphore_signal(barrier, inc=1, device_id=z_peer(i)[1], device_id_type=MESH)
    source_x = z // 2
    for zs in range(8):
        @pl.when(jnp.logical_and(zs != z, source_x != x))
        def _():
            pl.semaphore_signal(barrier, inc=1, device_id=ids(zs * 8 + v, source_x), device_id_type=MESH)

    @pl.when(source_x == x)
    def _():
        pl.semaphore_wait(barrier, 41)

    @pl.when(source_x != x)
    def _():
        pl.semaphore_wait(barrier, 44)

    def remote(src, dst, ssem, rsem, device):
        return pltpu.make_async_remote_copy(src_ref=src, dst_ref=dst, send_sem=ssem, recv_sem=rsem,
                                            device_id=device, device_id_type=MESH)

    def gram_out(i, carry):
        w, device = group_peer(i)
        remote(gp_ref.at[w], gin.at[u], gss.at[i], grs.at[i], device).start()
        return carry

    lax.fori_loop(1, 32, gram_out, 0)

    def v_peer(i):
        w = lax.rem(v + i, 8)
        return w, ids(z * 8 + w, x)

    coeff_sends = []
    for i in range(1, 8):
        w, device = v_peer(i)
        copy = remote(ct_ref.at[w], cin.at[v], css.at[i], crs.at[i], device)
        copy.start()
        coeff_sends.append(copy)
    cin[v] = ct_ref[v]
    gin[u] = gp_ref[u]

    def gram_in(i, carry):
        remote(gp_ref.at[0], gin.at[0], gss.at[i], grs.at[i], ids(node, x)).wait_recv()
        return carry

    lax.fori_loop(1, 32, gram_in, 0)
    total = gin[0]
    for w in range(1, 32):
        total = total + gin[w]
    part[...] = total

    z_sends = []
    for i in range(1, 8):
        w, device = z_peer(i)
        copy = remote(part, zin.at[z], zss.at[i], zrs.at[i], device)
        copy.start()
        z_sends.append(copy)
    zin[z] = total

    for copy in coeff_sends:
        copy.wait_recv()
    small = cin[0]
    for w in range(1, 8):
        small = small + cin[w]
    csum[...] = small.reshape(8, 8, R)

    for t in range(8):
        zl, s = t // 4, t % 4
        zt = 2 * x + zl
        mine = jnp.logical_and(zt == z, x == s)

        @pl.when(jnp.logical_not(mine))
        def _():
            remote(csum.at[t], cz.at[z], dss.at[t], drs.at[z], ids(zt * 8 + v, s)).start()

        @pl.when(mine)
        def _():
            cz[z] = csum[t]

    for copy in z_sends:
        copy.wait_recv()
    total = zin[0]
    for w in range(1, 8):
        total = total + zin[w]
    gfull_ref[u] = total

    def share(i, carry):
        w, device = group_peer(i)
        remote(gfull_ref.at[u], gfull_ref.at[u], ass.at[i], ars.at[i], device).start()
        return carry

    lax.fori_loop(1, 32, share, 0)

    for zs in range(8):
        @pl.when(jnp.logical_or(zs != z, source_x != x))
        def _():
            remote(csum.at[0], cz.at[zs], dss.at[0], drs.at[zs], ids(node, x)).wait_recv()
    out = cz[0]
    for w in range(1, 8):
        out = out + cz[w]
    cred_ref[...] = out

    def shared_in(i, carry):
        remote(gfull_ref.at[0], gfull_ref.at[0], ass.at[i], ars.at[i], ids(node, x)).wait_recv()
        return carry

    lax.fori_loop(1, 32, shared_in, 0)

    def finish(i, carry):
        remote(gp_ref.at[0], gin.at[0], gss.at[i], grs.at[i], ids(node, x)).wait_send()
        remote(gfull_ref.at[0], gfull_ref.at[0], ass.at[i], ars.at[i], ids(node, x)).wait_send()
        return carry

    lax.fori_loop(1, 32, finish, 0)
    for copy in coeff_sends + z_sends:
        copy.wait_send()
    for t in range(8):
        zl, s = t // 4, t % 4
        mine = jnp.logical_and(2 * x + zl == z, x == s)

        @pl.when(jnp.logical_not(mine))
        def _():
            remote(csum.at[t], cz.at[0], dss.at[t], drs.at[0], ids(node, x)).wait_send()


def factor_kernel(scale, g_ref, c_ref, y_ref, core_ref, next_ref, m_ref, inv_ref):
    lower = g_ref[0:20].reshape(R, 128) * scale
    m_ref[:, 0:128] = lower
    m_ref[0:128, 128:160] = lower[128:160, :].T
    m_ref[128:160, 128:160] = g_ref[20:24].reshape(32, 128)[:, 0:32] * scale
    lane = lax.broadcasted_iota(jnp.int32, (1, R), 1)
    lanes = lax.broadcasted_iota(jnp.int32, (PANEL, R), 1)
    row_id = lax.broadcasted_iota(jnp.int32, (PANEL, 1), 0)
    for p in range(R // PANEL):
        base = p * PANEL
        block = m_ref[base:base + PANEL, :]
        dinv = jnp.zeros((PANEL, 1), F32)
        for t in range(PANEL):
            k = base + t
            row = block[t:t + 1, :]
            inverse = 1.0 / block[t:t + 1, k:k + 1]
            dinv = jnp.where(row_id == t, inverse, dinv)
            if t + 1 < PANEL:
                col = jnp.where(row_id > t, block[:, k:k + 1] * inverse, 0.0)
                block = block - col * jnp.where(lane == k, row + 1.0, row)
        rows = lax.broadcasted_iota(jnp.int32, (PANEL, R), 0) + base
        unit = jnp.where(lanes < rows, block, jnp.where(lanes == rows, 1.0, 0.0))
        inv_ref[base:base + PANEL, :] = unit * jnp.sqrt(dinv)
        if base + PANEL < R:
            inside = (lanes >= base) & (lanes < base + PANEL)
            rest = jnp.where(inside, unit, block)
            update = lax.dot_general(block * dinv, rest, (((0,), (0,)), ((), ())),
                                     precision=HIGH, preferred_element_type=F32)
            below = slice(base + PANEL, R)
            keep = jnp.where((lane >= base) & (lane < base + PANEL), 0.0, m_ref[below, :])
            m_ref[below, :] = keep - update[below, :]
    inv = inv_ref[...]
    core_ref[...] = jnp.dot(inv, y_ref[...], precision=HIGH, preferred_element_type=F32)
    next_ref[...] = lax.dot_general(c_ref[...] * scale, inv, NT, precision=HIGH, preferred_element_type=F32)


def body(snapshots, sketch_matrix):
    node_total = snapshots.shape[0] * lax.axis_size("node")
    vmem = pl.BlockSpec(memory_space=pltpu.VMEM)
    dma = pltpu.SemaphoreType.DMA
    shape = jax.ShapeDtypeStruct
    y, gp, ct = pl.pallas_call(
        sketch_kernel,
        out_shape=(shape((R, 2048), F32), shape((32, 8, 128), F32), shape((8, 64, R), F32)),
        in_specs=[pl.BlockSpec(memory_space=pl.ANY), vmem],
        out_specs=(vmem, vmem, vmem),
        scratch_shapes=[
            pltpu.VMEM((16, PC, PC), BF16),
            pltpu.VMEM((6, R, PC), F32), pltpu.VMEM((6, R, PC), F32),
            pltpu.VMEM((6, R, PC), F32), pltpu.VMEM((6, R, PC), F32),
            pltpu.VMEM((4, R, PC), BF16), pltpu.VMEM((4, R, PC), BF16),
            pltpu.VMEM((4, R, PC), BF16), pltpu.VMEM((4, R, PC), BF16),
            pltpu.VMEM((R, PC), F32), pltpu.VMEM((R, R), F32),
            dma((16,)), dma((6,)), dma((6,)), dma((6,)), dma((6,)),
            dma((4,)), dma((4,)), dma((4,)), dma((4,)),
            dma((2,)), dma((2,)), dma((2,)), dma((2,)),
        ],
        compiler_params=pltpu.CompilerParams(collective_id=0, has_side_effects=True),
    )(snapshots, sketch_matrix.T)
    gfull, cred = pl.pallas_call(
        reduce_kernel,
        out_shape=(shape((32, 8, 128), F32), shape((8, R), F32)),
        in_specs=[vmem, vmem],
        out_specs=(vmem, vmem),
        scratch_shapes=[
            pltpu.VMEM((32, 8, 128), F32), pltpu.VMEM((8, 128), F32), pltpu.VMEM((8, 8, 128), F32),
            pltpu.VMEM((8, 64, R), F32), pltpu.VMEM((8, 8, R), F32), pltpu.VMEM((8, 8, R), F32),
            dma((32,)), dma((32,)), dma((8,)), dma((8,)), dma((32,)), dma((32,)),
            dma((8,)), dma((8,)), dma((8,)), dma((8,)),
        ],
        compiler_params=pltpu.CompilerParams(collective_id=1, has_side_effects=True),
    )(gp, ct)
    core, nxt = pl.pallas_call(
        functools.partial(factor_kernel, 1.0 / node_total),
        out_shape=(shape((R, 2048), F32), shape((8, R), F32)),
        in_specs=[vmem] * 3,
        out_specs=(vmem, vmem),
        scratch_shapes=[pltpu.VMEM((R, R), F32), pltpu.VMEM((R, R), F32)],
    )(gfull, cred, y)
    return core.T, nxt.T


def solution(mesh):
    placed = (P("node", "samp"), P("samp", None))
    return jax.shard_map(
        body,
        mesh=mesh,
        in_specs=placed,
        out_specs=(P(("node", "samp"), None), P("node", "samp")),
        check_vma=False,
    )
```

```python
import functools
import jax
import jax.numpy as jnp
from jax import lax
from jax.experimental import pallas as pl
from jax.experimental.pallas import tpu as pltpu
from jax.sharding import PartitionSpec as P

MESH = pl.DeviceIdType.MESH
HIGH = lax.Precision.HIGHEST
R = 160
PC = 512
NT = (((1,), (1,)), ((), ()))
F32 = jnp.float32
BF16 = jnp.bfloat16
PANEL = 32
TOP = 230.0


def encode(value, code_ref, peak_ref, k):
    parts = [value[:, i:i + 128].reshape(R // 8, 8, 128) for i in range(0, PC, 128)]
    peak = jnp.maximum(jnp.max(jnp.abs(parts[0]), axis=0), 1e-30)
    for part in parts[1:]:
        peak = jnp.maximum(peak, jnp.max(jnp.abs(part), axis=0))
    peak_ref[k] = peak
    gain = TOP / peak
    for i, part in enumerate(parts):
        scaled = part * gain
        power = scaled * scaled
        power = power * power
        power = power * power
        power = power * power
        power = jnp.where(scaled < 0.0, -power, power)
        code_ref[k, :, i * 128:(i + 1) * 128] = power.reshape(R, 128).astype(BF16)


def decode(code_ref, peak_ref, k):
    gain = peak_ref[k] * (1.0 / TOP)
    out = []
    for i in range(0, PC, 128):
        power = code_ref[k, :, i:i + 128].astype(F32)
        root = lax.rsqrt(lax.rsqrt(lax.rsqrt(lax.rsqrt(jnp.abs(power)))))
        root = jnp.where(power < 0.0, -root, root).reshape(R // 8, 8, 128) * gain
        out.append(root.reshape(R, 128))
    return jnp.concatenate(out, axis=1)


def sketch_kernel(s_hbm, om_ref, y_ref, gp_ref, ct_ref,
                  sv, sl, sr, rl, rr, slp, srp, rlp, rrp, held, yown, yr, yl, yopp, cacc, gacc,
                  load_sem, sls, srs, rls, rrs, slps, srps, rlps, rrps, gsl, gsr, grr, grl, fsl, fsr, frr, frl):
    me = lax.axis_index("samp")
    left = lax.rem(me + 3, 4)
    right = lax.rem(me + 1, 4)
    opp = lax.rem(me + 2, 4)

    barrier = pltpu.get_barrier_semaphore()
    for peer in (left, right):
        pl.semaphore_signal(barrier, inc=1, device_id={"samp": peer}, device_id_type=MESH)

    order = [(opp, 0), (opp, 2), (opp, 1), (opp, 3),
             (left, 2), (right, 0), (left, 3), (right, 1),
             (left, 0), (right, 2), (left, 1), (right, 3),
             (me, 0), (me, 2), (me, 1), (me, 3)]
    where = {"opp": [0, 2, 1, 3], "left": [8, 10, 4, 6], "right": [5, 7, 9, 11], "me": [12, 14, 13, 15]}

    loads = []
    for pos, (chunk, piece) in enumerate(order):
        start = pl.multiple_of(chunk * 2048 + piece * PC, PC)
        copy = pltpu.make_async_copy(s_hbm.at[pl.ds(start, PC), :], sv.at[pos], load_sem.at[pos])
        copy.start()
        loads.append(copy)

    def sketch(pos):
        loads[pos].wait()
        return lax.dot_general(om_ref[...], sv[pos], NT, preferred_element_type=F32)

    def send(src, dst, ssem, rsem, peer):
        copy = pltpu.make_async_remote_copy(src_ref=src, dst_ref=dst, send_sem=ssem, recv_sem=rsem,
                                            device_id={"samp": peer}, device_id_type=MESH)
        copy.start()
        return copy

    to_left = [None] * 6
    to_right = [None] * 6

    def send_left(k):
        to_left[k] = (send(sl.at[k], rr.at[k], sls.at[k], rrs.at[k], left),
                      send(slp.at[k], rrp.at[k], slps.at[k], rrps.at[k], left))

    def send_right(k):
        to_right[k] = (send(sr.at[k], rl.at[k], srs.at[k], rls.at[k], right),
                       send(srp.at[k], rlp.at[k], srps.at[k], rlps.at[k], right))

    def from_right(k):
        for copy in to_left[k]:
            copy.wait_recv()
        return decode(rr, rrp, k)

    def from_left(k):
        for copy in to_right[k]:
            copy.wait_recv()
        return decode(rl, rlp, k)

    encode(sketch(0), sl, slp, 0)
    encode(sketch(1), sr, srp, 0)
    pl.semaphore_wait(barrier, 2)
    send_left(0)
    send_right(0)
    for k, (a, b) in enumerate([(2, 3), (4, 5), (6, 7)]):
        encode(sketch(a), sl, slp, k + 1)
        send_left(k + 1)
        encode(sketch(b), sr, srp, k + 1)
        send_right(k + 1)
    for k in range(2):
        held[2 * k] = sketch(8 + 2 * k)
        held[2 * k + 1] = sketch(9 + 2 * k)
    for pos, piece in ((12, 0), (13, 2), (14, 1), (15, 3)):
        y_ref[:, piece * PC:(piece + 1) * PC] = sketch(pos)

    for k in range(2):
        encode(held[2 * k] + from_right(k), sl, slp, 4 + k)
        send_left(4 + k)
        encode(held[2 * k + 1] + from_left(k), sr, srp, 4 + k)
        send_right(4 + k)

    for k in range(2):
        y_ref[:, k * PC:(k + 1) * PC] += from_left(2 + k)
        y_ref[:, (2 + k) * PC:(3 + k) * PC] += from_right(2 + k)

    gather_left = [None] * 4
    gather_right = [None] * 4

    def finish(piece, last, first):
        columns = slice(piece * PC, (piece + 1) * PC)
        value = y_ref[:, columns] + last
        y_ref[:, columns] = value
        rounded = value.astype(BF16)
        yown[piece] = rounded
        gather_left[piece] = send(yown.at[piece], yr.at[piece], gsl.at[piece], grr.at[piece], left)
        gather_right[piece] = send(yown.at[piece], yl.at[piece], gsr.at[piece], grl.at[piece], right)
        gram = lax.dot_general(value, value, NT, precision=HIGH, preferred_element_type=F32)
        coeff = jnp.dot(rounded, sv[where["me"][piece]], preferred_element_type=F32)
        if first:
            gacc[...] = gram
            cacc[...] = coeff
        else:
            gacc[...] += gram
            cacc[...] += coeff

    finish(0, from_right(4), True)
    finish(2, from_left(4), False)
    finish(1, from_right(5), False)
    finish(3, from_left(5), False)

    gram = gacc[...]
    gp_ref[0:20] = gram[:, 0:128].reshape(20, 8, 128)
    gp_ref[20:32] = jnp.zeros((12, 8, 128), F32)
    gp_ref[20:24, :, 0:32] = gram[128:160, 128:160].reshape(4, 8, 32)

    forward = [None] * 4
    for piece in (0, 2, 1, 3):
        gather_left[piece].wait_recv()
        if piece in (0, 2):
            forward[piece] = send(yr.at[piece], yopp.at[piece], fsl.at[piece // 2], frr.at[piece // 2], left)
        gather_right[piece].wait_recv()
        if piece in (1, 3):
            forward[piece] = send(yl.at[piece], yopp.at[piece], fsr.at[piece // 2], frl.at[piece // 2], right)
        cacc[...] += jnp.dot(yr[piece], sv[where["right"][piece]], preferred_element_type=F32)
        cacc[...] += jnp.dot(yl[piece], sv[where["left"][piece]], preferred_element_type=F32)
    for piece in (0, 2, 1, 3):
        forward[piece].wait_recv()
        cacc[...] += jnp.dot(yopp[piece], sv[where["opp"][piece]], preferred_element_type=F32)

    turned = cacc[...].T
    for zl in range(2):
        for v in range(8):
            ct_ref[v, zl * 32:(zl + 1) * 32, :] = turned[(zl * 8 + v) * 32:(zl * 8 + v + 1) * 32, :]

    for pair in to_left + to_right:
        pair[0].wait_send()
        pair[1].wait_send()
    for copy in gather_left + gather_right + forward:
        copy.wait_send()


def reduce_kernel(gp_ref, ct_ref, gfull_ref, cred_ref, gin, part, zin, cin, csum, cz,
                  gss, grs, zss, zrs, ass, ars, css, crs, dss, drs):
    node = lax.axis_index("node")
    x = lax.axis_index("samp")
    z = node // 8
    v = lax.rem(node, 8)
    u = x * 8 + v

    barrier = pltpu.get_barrier_semaphore()

    def ids(node_to, samp_to):
        return {"node": node_to, "samp": samp_to}

    def group_peer(i):
        w = lax.rem(u + i, 32)
        return w, ids(z * 8 + lax.rem(w, 8), w // 8)

    def z_peer(i):
        w = lax.rem(z + i, 8)
        return w, ids(w * 8 + v, x)

    def greet(i, carry):
        pl.semaphore_signal(barrier, inc=1, device_id=group_peer(i)[1], device_id_type=MESH)
        return carry

    lax.fori_loop(1, 32, greet, 0)
    for i in range(1, 8):
        pl.semaphore_signal(barrier, inc=1, device_id=z_peer(i)[1], device_id_type=MESH)
    source_x = z // 2
    for zs in range(8):
        @pl.when(jnp.logical_and(zs != z, source_x != x))
        def _():
            pl.semaphore_signal(barrier, inc=1, device_id=ids(zs * 8 + v, source_x), device_id_type=MESH)

    @pl.when(source_x == x)
    def _():
        pl.semaphore_wait(barrier, 41)

    @pl.when(source_x != x)
    def _():
        pl.semaphore_wait(barrier, 44)

    def remote(src, dst, ssem, rsem, device):
        return pltpu.make_async_remote_copy(src_ref=src, dst_ref=dst, send_sem=ssem, recv_sem=rsem,
                                            device_id=device, device_id_type=MESH)

    def gram_out(i, carry):
        w, device = group_peer(i)
        remote(gp_ref.at[w], gin.at[u], gss.at[i], grs.at[i], device).start()
        return carry

    lax.fori_loop(1, 32, gram_out, 0)

    def v_peer(i):
        w = lax.rem(v + i, 8)
        return w, ids(z * 8 + w, x)

    coeff_sends = []
    for i in range(1, 8):
        w, device = v_peer(i)
        copy = remote(ct_ref.at[w], cin.at[v], css.at[i], crs.at[i], device)
        copy.start()
        coeff_sends.append(copy)
    cin[v] = ct_ref[v]
    gin[u] = gp_ref[u]

    def gram_in(i, carry):
        remote(gp_ref.at[0], gin.at[0], gss.at[i], grs.at[i], ids(node, x)).wait_recv()
        return carry

    lax.fori_loop(1, 32, gram_in, 0)
    total = gin[0]
    for w in range(1, 32):
        total = total + gin[w]
    part[...] = total

    z_sends = []
    for i in range(1, 8):
        w, device = z_peer(i)
        copy = remote(part, zin.at[z], zss.at[i], zrs.at[i], device)
        copy.start()
        z_sends.append(copy)
    zin[z] = total

    for copy in coeff_sends:
        copy.wait_recv()
    small = cin[0]
    for w in range(1, 8):
        small = small + cin[w]
    csum[...] = small.reshape(8, 8, R)

    for t in range(8):
        zl, s = t // 4, t % 4
        zt = 2 * x + zl
        mine = jnp.logical_and(zt == z, x == s)

        @pl.when(jnp.logical_not(mine))
        def _():
            remote(csum.at[t], cz.at[z], dss.at[t], drs.at[z], ids(zt * 8 + v, s)).start()

        @pl.when(mine)
        def _():
            cz[z] = csum[t]

    for copy in z_sends:
        copy.wait_recv()
    total = zin[0]
    for w in range(1, 8):
        total = total + zin[w]
    gfull_ref[u] = total

    def share(i, carry):
        w, device = group_peer(i)
        remote(gfull_ref.at[u], gfull_ref.at[u], ass.at[i], ars.at[i], device).start()
        return carry

    lax.fori_loop(1, 32, share, 0)

    for zs in range(8):
        @pl.when(jnp.logical_or(zs != z, source_x != x))
        def _():
            remote(csum.at[0], cz.at[zs], dss.at[0], drs.at[zs], ids(node, x)).wait_recv()
    out = cz[0]
    for w in range(1, 8):
        out = out + cz[w]
    cred_ref[...] = out

    def shared_in(i, carry):
        remote(gfull_ref.at[0], gfull_ref.at[0], ass.at[i], ars.at[i], ids(node, x)).wait_recv()
        return carry

    lax.fori_loop(1, 32, shared_in, 0)

    def finish(i, carry):
        remote(gp_ref.at[0], gin.at[0], gss.at[i], grs.at[i], ids(node, x)).wait_send()
        remote(gfull_ref.at[0], gfull_ref.at[0], ass.at[i], ars.at[i], ids(node, x)).wait_send()
        return carry

    lax.fori_loop(1, 32, finish, 0)
    for copy in coeff_sends + z_sends:
        copy.wait_send()
    for t in range(8):
        zl, s = t // 4, t % 4
        mine = jnp.logical_and(2 * x + zl == z, x == s)

        @pl.when(jnp.logical_not(mine))
        def _():
            remote(csum.at[t], cz.at[0], dss.at[t], drs.at[0], ids(node, x)).wait_send()


def factor_kernel(scale, g_ref, c_ref, y_ref, core_ref, next_ref, m_ref, inv_ref):
    lower = g_ref[0:20].reshape(R, 128) * scale
    m_ref[:, 0:128] = lower
    m_ref[0:128, 128:160] = lower[128:160, :].T
    m_ref[128:160, 128:160] = g_ref[20:24].reshape(32, 128)[:, 0:32] * scale
    lane = lax.broadcasted_iota(jnp.int32, (1, R), 1)
    lanes = lax.broadcasted_iota(jnp.int32, (PANEL, R), 1)
    row_id = lax.broadcasted_iota(jnp.int32, (PANEL, 1), 0)
    for p in range(R // PANEL):
        base = p * PANEL
        block = m_ref[base:base + PANEL, :]
        dinv = jnp.zeros((PANEL, 1), F32)
        for t in range(PANEL):
            k = base + t
            row = block[t:t + 1, :]
            inverse = 1.0 / block[t:t + 1, k:k + 1]
            dinv = jnp.where(row_id == t, inverse, dinv)
            if t + 1 < PANEL:
                col = jnp.where(row_id > t, block[:, k:k + 1] * inverse, 0.0)
                block = block - col * jnp.where(lane == k, row + 1.0, row)
        rows = lax.broadcasted_iota(jnp.int32, (PANEL, R), 0) + base
        unit = jnp.where(lanes < rows, block, jnp.where(lanes == rows, 1.0, 0.0))
        inv_ref[base:base + PANEL, :] = unit * jnp.sqrt(dinv)
        if base + PANEL < R:
            inside = (lanes >= base) & (lanes < base + PANEL)
            rest = jnp.where(inside, unit, block)
            update = lax.dot_general(block * dinv, rest, (((0,), (0,)), ((), ())),
                                     precision=HIGH, preferred_element_type=F32)
            below = slice(base + PANEL, R)
            keep = jnp.where((lane >= base) & (lane < base + PANEL), 0.0, m_ref[below, :])
            m_ref[below, :] = keep - update[below, :]
    inv = inv_ref[...]
    core_ref[...] = jnp.dot(inv, y_ref[...], precision=HIGH, preferred_element_type=F32)
    next_ref[...] = lax.dot_general(c_ref[...] * scale, inv, NT, precision=HIGH, preferred_element_type=F32)


def body(snapshots, sketch_matrix):
    node_total = snapshots.shape[0] * lax.axis_size("node")
    vmem = pl.BlockSpec(memory_space=pltpu.VMEM)
    dma = pltpu.SemaphoreType.DMA
    shape = jax.ShapeDtypeStruct
    y, gp, ct = pl.pallas_call(
        sketch_kernel,
        out_shape=(shape((R, 2048), F32), shape((32, 8, 128), F32), shape((8, 64, R), F32)),
        in_specs=[pl.BlockSpec(memory_space=pl.ANY), vmem],
        out_specs=(vmem, vmem, vmem),
        scratch_shapes=[
            pltpu.VMEM((16, PC, PC), BF16),
            pltpu.VMEM((6, R, PC), BF16), pltpu.VMEM((6, R, PC), BF16),
            pltpu.VMEM((6, R, PC), BF16), pltpu.VMEM((6, R, PC), BF16),
            pltpu.VMEM((6, 8, 128), F32), pltpu.VMEM((6, 8, 128), F32),
            pltpu.VMEM((6, 8, 128), F32), pltpu.VMEM((6, 8, 128), F32),
            pltpu.VMEM((4, R, PC), F32),
            pltpu.VMEM((4, R, PC), BF16), pltpu.VMEM((4, R, PC), BF16),
            pltpu.VMEM((4, R, PC), BF16), pltpu.VMEM((4, R, PC), BF16),
            pltpu.VMEM((R, PC), F32), pltpu.VMEM((R, R), F32),
            dma((16,)), dma((6,)), dma((6,)), dma((6,)), dma((6,)),
            dma((6,)), dma((6,)), dma((6,)), dma((6,)),
            dma((4,)), dma((4,)), dma((4,)), dma((4,)),
            dma((2,)), dma((2,)), dma((2,)), dma((2,)),
        ],
        compiler_params=pltpu.CompilerParams(collective_id=0, has_side_effects=True),
    )(snapshots, sketch_matrix.T)
    gfull, cred = pl.pallas_call(
        reduce_kernel,
        out_shape=(shape((32, 8, 128), F32), shape((8, R), F32)),
        in_specs=[vmem, vmem],
        out_specs=(vmem, vmem),
        scratch_shapes=[
            pltpu.VMEM((32, 8, 128), F32), pltpu.VMEM((8, 128), F32), pltpu.VMEM((8, 8, 128), F32),
            pltpu.VMEM((8, 64, R), F32), pltpu.VMEM((8, 8, R), F32), pltpu.VMEM((8, 8, R), F32),
            dma((32,)), dma((32,)), dma((8,)), dma((8,)), dma((32,)), dma((32,)),
            dma((8,)), dma((8,)), dma((8,)), dma((8,)),
        ],
        compiler_params=pltpu.CompilerParams(collective_id=1, has_side_effects=True),
    )(gp, ct)
    core, nxt = pl.pallas_call(
        functools.partial(factor_kernel, 1.0 / node_total),
        out_shape=(shape((R, 2048), F32), shape((8, R), F32)),
        in_specs=[vmem] * 3,
        out_specs=(vmem, vmem),
        scratch_shapes=[pltpu.VMEM((R, R), F32), pltpu.VMEM((R, R), F32)],
    )(gfull, cred, y)
    return core.T, nxt.T


def solution(mesh):
    placed = (P("node", "samp"), P("samp", None))
    return jax.shard_map(
        body,
        mesh=mesh,
        in_specs=placed,
        out_specs=(P(("node", "samp"), None), P("node", "samp")),
        check_vma=False,
    )
```

```python
import functools
import jax
import jax.numpy as jnp
from jax import lax
from jax.experimental import pallas as pl
from jax.experimental.pallas import tpu as pltpu
from jax.sharding import PartitionSpec as P

MESH = pl.DeviceIdType.MESH
HIGH = lax.Precision.HIGHEST
R = 160
PC = 512
NT = (((1,), (1,)), ((), ()))
F32 = jnp.float32
BF16 = jnp.bfloat16
PANEL = 32
TOP = 230.0


def encode(value, code_ref, peak_ref, k):
    parts = [value[:, i:i + 128].reshape(R // 8, 8, 128) for i in range(0, PC, 128)]
    peak = jnp.maximum(jnp.max(jnp.abs(parts[0]), axis=0), 1e-30)
    for part in parts[1:]:
        peak = jnp.maximum(peak, jnp.max(jnp.abs(part), axis=0))
    peak_ref[k] = peak
    gain = TOP / peak
    for i, part in enumerate(parts):
        scaled = part * gain
        power = scaled * scaled
        power = power * power
        power = power * power
        power = power * power
        power = jnp.where(scaled < 0.0, -power, power)
        code_ref[k, :, i * 128:(i + 1) * 128] = power.reshape(R, 128).astype(BF16)


def decode(code_ref, peak_ref, k):
    gain = peak_ref[k] * (1.0 / TOP)
    out = []
    for i in range(0, PC, 128):
        power = code_ref[k, :, i:i + 128].astype(F32)
        root = lax.rsqrt(lax.rsqrt(lax.rsqrt(lax.rsqrt(jnp.abs(power)))))
        root = jnp.where(power < 0.0, -root, root).reshape(R // 8, 8, 128) * gain
        out.append(root.reshape(R, 128))
    return jnp.concatenate(out, axis=1)


def fused_kernel(scale, s_hbm, om_ref, core_ref, next_ref,
                 sv, sl, sr, rl, rr, slp, srp, rlp, rrp, held, y_ref, yown, yr, yl, yopp, cacc, gacc,
                 gp, gin, part, zin, gfull, cp, cin, csum, cz, m_ref, inv_ref,
                 load_sem, sls, srs, rls, rrs, slps, srps, rlps, rrps,
                 gsl, gsr, grr, grl, fsl, fsr, frr, frl,
                 gss, grs, zss, zrs, ass, ars, css, crs, dss, drs):
    node = lax.axis_index("node")
    me = lax.axis_index("samp")
    z = node // 8
    v = lax.rem(node, 8)
    u = me * 8 + v
    left = lax.rem(me + 3, 4)
    right = lax.rem(me + 1, 4)
    opp = lax.rem(me + 2, 4)

    def ids(node_to, samp_to):
        return {"node": node_to, "samp": samp_to}

    def group_peer(i):
        w = lax.rem(u + i, 32)
        return w, ids(z * 8 + lax.rem(w, 8), w // 8)

    def z_peer(i):
        w = lax.rem(z + i, 8)
        return w, ids(w * 8 + v, me)

    def v_peer(i):
        w = lax.rem(v + i, 8)
        return w, ids(z * 8 + w, me)

    order = [(opp, 0), (opp, 2), (opp, 1), (opp, 3),
             (left, 2), (right, 0), (left, 3), (right, 1),
             (left, 0), (right, 2), (left, 1), (right, 3),
             (me, 0), (me, 2), (me, 1), (me, 3)]
    where = {"opp": [0, 2, 1, 3], "left": [8, 10, 4, 6], "right": [5, 7, 9, 11], "me": [12, 14, 13, 15]}
    loads = []
    for pos, (chunk, piece) in enumerate(order):
        start = pl.multiple_of(chunk * 2048 + piece * PC, PC)
        copy = pltpu.make_async_copy(s_hbm.at[pl.ds(start, PC), :], sv.at[pos], load_sem.at[pos])
        copy.start()
        loads.append(copy)

    barrier = pltpu.get_barrier_semaphore()

    def greet(i, carry):
        pl.semaphore_signal(barrier, inc=1, device_id=group_peer(i)[1], device_id_type=MESH)
        return carry

    lax.fori_loop(1, 32, greet, 0)
    for i in range(1, 8):
        pl.semaphore_signal(barrier, inc=1, device_id=z_peer(i)[1], device_id_type=MESH)
    source_x = z // 2
    for zs in range(8):
        @pl.when(jnp.logical_and(zs != z, source_x != me))
        def _():
            pl.semaphore_signal(barrier, inc=1, device_id=ids(zs * 8 + v, source_x), device_id_type=MESH)

    def sketch(pos):
        loads[pos].wait()
        return lax.dot_general(om_ref[...], sv[pos], NT, preferred_element_type=F32)

    def remote(src, dst, ssem, rsem, device):
        return pltpu.make_async_remote_copy(src_ref=src, dst_ref=dst, send_sem=ssem, recv_sem=rsem,
                                            device_id=device, device_id_type=MESH)

    def send(src, dst, ssem, rsem, peer):
        copy = remote(src, dst, ssem, rsem, {"samp": peer})
        copy.start()
        return copy

    to_left = [None] * 6
    to_right = [None] * 6

    def send_left(k):
        to_left[k] = (send(sl.at[k], rr.at[k], sls.at[k], rrs.at[k], left),
                      send(slp.at[k], rrp.at[k], slps.at[k], rrps.at[k], left))

    def send_right(k):
        to_right[k] = (send(sr.at[k], rl.at[k], srs.at[k], rls.at[k], right),
                       send(srp.at[k], rlp.at[k], srps.at[k], rlps.at[k], right))

    def from_right(k):
        for copy in to_left[k]:
            copy.wait_recv()
        return decode(rr, rrp, k)

    def from_left(k):
        for copy in to_right[k]:
            copy.wait_recv()
        return decode(rl, rlp, k)

    encode(sketch(0), sl, slp, 0)
    encode(sketch(1), sr, srp, 0)

    @pl.when(source_x == me)
    def _():
        pl.semaphore_wait(barrier, 41)

    @pl.when(source_x != me)
    def _():
        pl.semaphore_wait(barrier, 44)

    send_left(0)
    send_right(0)
    for k, (a, b) in enumerate([(2, 3), (4, 5), (6, 7)]):
        encode(sketch(a), sl, slp, k + 1)
        send_left(k + 1)
        encode(sketch(b), sr, srp, k + 1)
        send_right(k + 1)
    for k in range(2):
        held[2 * k] = sketch(8 + 2 * k)
        held[2 * k + 1] = sketch(9 + 2 * k)
    for pos, piece in ((12, 0), (13, 2), (14, 1), (15, 3)):
        y_ref[:, piece * PC:(piece + 1) * PC] = sketch(pos)

    for k in range(2):
        encode(held[2 * k] + from_right(k), sl, slp, 4 + k)
        send_left(4 + k)
        encode(held[2 * k + 1] + from_left(k), sr, srp, 4 + k)
        send_right(4 + k)

    for k in range(2):
        y_ref[:, k * PC:(k + 1) * PC] += from_left(2 + k)
        y_ref[:, (2 + k) * PC:(3 + k) * PC] += from_right(2 + k)

    gather_left = [None] * 4
    gather_right = [None] * 4

    def finish(piece, last):
        columns = slice(piece * PC, (piece + 1) * PC)
        value = y_ref[:, columns] + last
        y_ref[:, columns] = value
        yown[piece] = value.astype(BF16)
        gram = lax.dot_general(value, value, NT, precision=HIGH, preferred_element_type=F32)
        if piece == 0:
            gacc[...] = gram
        else:
            gacc[...] += gram

    def gather(piece):
        gather_left[piece] = send(yown.at[piece], yr.at[piece], gsl.at[piece], grr.at[piece], left)
        gather_right[piece] = send(yown.at[piece], yl.at[piece], gsr.at[piece], grl.at[piece], right)

    finish(0, from_right(4))
    gather(0)
    finish(2, from_left(4))
    gather(2)
    finish(1, from_right(5))
    finish(3, from_left(5))

    gram = gacc[...]
    gp[0:20] = gram[:, 0:128].reshape(20, 8, 128)
    gp[20:32] = jnp.zeros((12, 8, 128), F32)
    gp[20:24, :, 0:32] = gram[128:160, 128:160].reshape(4, 8, 32)

    def gram_out(i, carry):
        w, device = group_peer(i)
        remote(gp.at[w], gin.at[u], gss.at[i], grs.at[i], device).start()
        return carry

    lax.fori_loop(1, 32, gram_out, 0)
    gather(1)
    gather(3)
    gin[u] = gp[u]

    def coeff(rows, name, piece):
        return jnp.dot(rows, sv[where[name][piece]], preferred_element_type=F32)

    cacc[...] = coeff(yown[0], "me", 0)
    for piece in (2, 1, 3):
        cacc[...] += coeff(yown[piece], "me", piece)

    def gram_in(i, carry):
        remote(gp.at[0], gin.at[0], gss.at[i], grs.at[i], ids(node, me)).wait_recv()
        return carry

    lax.fori_loop(1, 32, gram_in, 0)
    total = gin[0]
    for w in range(1, 32):
        total = total + gin[w]
    part[...] = total
    z_sends = []
    for i in range(1, 8):
        w, device = z_peer(i)
        copy = remote(part, zin.at[z], zss.at[i], zrs.at[i], device)
        copy.start()
        z_sends.append(copy)
    zin[z] = total

    def sides(piece):
        gather_left[piece].wait_recv()
        cacc[...] += coeff(yr[piece], "right", piece)
        gather_right[piece].wait_recv()
        cacc[...] += coeff(yl[piece], "left", piece)

    sides(0)
    sides(2)

    for copy in z_sends:
        copy.wait_recv()
    total = zin[0]
    for w in range(1, 8):
        total = total + zin[w]
    gfull[u] = total

    def share(i, carry):
        w, device = group_peer(i)
        remote(gfull.at[u], gfull.at[u], ass.at[i], ars.at[i], device).start()
        return carry

    lax.fori_loop(1, 32, share, 0)

    forward = [None] * 4

    def relay(piece):
        if piece in (0, 2):
            forward[piece] = send(yr.at[piece], yopp.at[piece], fsl.at[piece // 2], frr.at[piece // 2], left)
        else:
            forward[piece] = send(yl.at[piece], yopp.at[piece], fsr.at[piece // 2], frl.at[piece // 2], right)

    relay(0)
    relay(2)
    sides(1)
    relay(1)
    sides(3)
    relay(3)

    def shared_in(i, carry):
        remote(gfull.at[0], gfull.at[0], ass.at[i], ars.at[i], ids(node, me)).wait_recv()
        return carry

    lax.fori_loop(1, 32, shared_in, 0)

    lower = gfull[0:20].reshape(R, 128) * scale
    m_ref[:, 0:128] = lower
    m_ref[0:128, 128:160] = lower[128:160, :].T
    m_ref[128:160, 128:160] = gfull[20:24].reshape(32, 128)[:, 0:32] * scale
    lane = lax.broadcasted_iota(jnp.int32, (1, R), 1)
    lanes = lax.broadcasted_iota(jnp.int32, (PANEL, R), 1)
    row_id = lax.broadcasted_iota(jnp.int32, (PANEL, 1), 0)

    def panel(p):
        base = p * PANEL
        block = m_ref[base:base + PANEL, :]
        dinv = jnp.zeros((PANEL, 1), F32)
        for t in range(PANEL):
            k = base + t
            row = block[t:t + 1, :]
            inverse = 1.0 / block[t:t + 1, k:k + 1]
            dinv = jnp.where(row_id == t, inverse, dinv)
            if t + 1 < PANEL:
                col = jnp.where(row_id > t, block[:, k:k + 1] * inverse, 0.0)
                block = block - col * jnp.where(lane == k, row + 1.0, row)
        rows = lax.broadcasted_iota(jnp.int32, (PANEL, R), 0) + base
        unit = jnp.where(lanes < rows, block, jnp.where(lanes == rows, 1.0, 0.0))
        inv_ref[base:base + PANEL, :] = unit * jnp.sqrt(dinv)
        if base + PANEL < R:
            inside = (lanes >= base) & (lanes < base + PANEL)
            rest = jnp.where(inside, unit, block)
            update = lax.dot_general(block * dinv, rest, (((0,), (0,)), ((), ())),
                                     precision=HIGH, preferred_element_type=F32)
            below = slice(base + PANEL, R)
            keep = jnp.where((lane >= base) & (lane < base + PANEL), 0.0, m_ref[below, :])
            m_ref[below, :] = keep - update[below, :]

    panel(0)
    panel(1)

    for piece in (0, 2, 1, 3):
        forward[piece].wait_recv()
        cacc[...] += coeff(yopp[piece], "opp", piece)
    top = cacc[0:128, :].T
    rest = cacc[128:160, :].T
    for w in range(8):
        for zl in range(2):
            start = (zl * 8 + w) * 32
            cp[w, zl * 32:(zl + 1) * 32, :] = top[start:start + 32, :]
            for h in range(2):
                g = zl * 2 + h
                cp[w, 64:80, g * 32:(g + 1) * 32] = rest[start + h * 16:start + h * 16 + 16, :]
    coeff_sends = []
    for i in range(1, 8):
        w, device = v_peer(i)
        copy = remote(cp.at[w], cin.at[v], css.at[i], crs.at[i], device)
        copy.start()
        coeff_sends.append(copy)
    cin[v] = cp[v]

    panel(2)
    panel(3)
    panel(4)

    for copy in coeff_sends:
        copy.wait_recv()
    small = cin[0]
    for w in range(1, 8):
        small = small + cin[w]
    for t in range(8):
        g, h = t // 2, t % 2
        csum[t, :, 0:128] = small[t * 8:t * 8 + 8, :]
        csum[t, :, 128:160] = small[64 + h * 8:72 + h * 8, g * 32:(g + 1) * 32]

    def mine(t):
        return jnp.logical_and(2 * me + t // 4 == z, me == t % 4)

    for t in range(8):
        @pl.when(jnp.logical_not(mine(t)))
        def _():
            remote(csum.at[t], cz.at[z], dss.at[t], drs.at[z], ids((2 * me + t // 4) * 8 + v, t % 4)).start()

        @pl.when(mine(t))
        def _():
            cz[z] = csum[t]

    inv = inv_ref[...]
    core_ref[...] = jnp.dot(inv, y_ref[...], precision=HIGH, preferred_element_type=F32)

    for zs in range(8):
        @pl.when(jnp.logical_or(zs != z, source_x != me))
        def _():
            remote(csum.at[0], cz.at[zs], dss.at[0], drs.at[zs], ids(node, me)).wait_recv()
    out = cz[0]
    for w in range(1, 8):
        out = out + cz[w]
    next_ref[...] = lax.dot_general(out * scale, inv, NT, precision=HIGH, preferred_element_type=F32)

    def drain(i, carry):
        remote(gp.at[0], gin.at[0], gss.at[i], grs.at[i], ids(node, me)).wait_send()
        remote(gfull.at[0], gfull.at[0], ass.at[i], ars.at[i], ids(node, me)).wait_send()
        return carry

    lax.fori_loop(1, 32, drain, 0)
    for pair in to_left + to_right:
        pair[0].wait_send()
        pair[1].wait_send()
    for copy in gather_left + gather_right + forward + coeff_sends + z_sends:
        copy.wait_send()
    for t in range(8):
        @pl.when(jnp.logical_not(mine(t)))
        def _():
            remote(csum.at[t], cz.at[0], dss.at[t], drs.at[0], ids(node, me)).wait_send()


def body(snapshots, sketch_matrix):
    node_total = snapshots.shape[0] * lax.axis_size("node")
    vmem = pl.BlockSpec(memory_space=pltpu.VMEM)
    dma = pltpu.SemaphoreType.DMA
    shape = jax.ShapeDtypeStruct
    scratch = pltpu.VMEM
    core, nxt = pl.pallas_call(
        functools.partial(fused_kernel, 1.0 / node_total),
        out_shape=(shape((R, 2048), F32), shape((8, R), F32)),
        in_specs=[pl.BlockSpec(memory_space=pl.ANY), vmem],
        out_specs=(vmem, vmem),
        scratch_shapes=[
            scratch((16, PC, PC), BF16),
            scratch((6, R, PC), BF16), scratch((6, R, PC), BF16),
            scratch((6, R, PC), BF16), scratch((6, R, PC), BF16),
            scratch((6, 8, 128), F32), scratch((6, 8, 128), F32),
            scratch((6, 8, 128), F32), scratch((6, 8, 128), F32),
            scratch((4, R, PC), F32), scratch((R, 2048), F32),
            scratch((4, R, PC), BF16), scratch((4, R, PC), BF16),
            scratch((4, R, PC), BF16), scratch((4, R, PC), BF16),
            scratch((R, PC), F32), scratch((R, R), F32),
            scratch((32, 8, 128), F32), scratch((32, 8, 128), F32), scratch((8, 128), F32),
            scratch((8, 8, 128), F32), scratch((32, 8, 128), F32),
            scratch((8, 80, 128), F32), scratch((8, 80, 128), F32),
            scratch((8, 8, R), F32), scratch((8, 8, R), F32),
            scratch((R, R), F32), scratch((R, R), F32),
            dma((16,)), dma((6,)), dma((6,)), dma((6,)), dma((6,)),
            dma((6,)), dma((6,)), dma((6,)), dma((6,)),
            dma((4,)), dma((4,)), dma((4,)), dma((4,)),
            dma((2,)), dma((2,)), dma((2,)), dma((2,)),
            dma((32,)), dma((32,)), dma((8,)), dma((8,)), dma((32,)), dma((32,)),
            dma((8,)), dma((8,)), dma((8,)), dma((8,)),
        ],
        compiler_params=pltpu.CompilerParams(collective_id=0, has_side_effects=True),
    )(snapshots, sketch_matrix.T)
    return core.T, nxt.T


def solution(mesh):
    placed = (P("node", "samp"), P("samp", None))
    return jax.shard_map(
        body,
        mesh=mesh,
        in_specs=placed,
        out_specs=(P(("node", "samp"), None), P("node", "samp")),
        check_vma=False,
    )
```

```python
import functools
import jax
import jax.numpy as jnp
from jax import lax
from jax.experimental import pallas as pl
from jax.experimental.pallas import tpu as pltpu
from jax.sharding import PartitionSpec as P

MESH = pl.DeviceIdType.MESH
HIGH = lax.Precision.HIGHEST
R = 160
PC = 512
NT = (((1,), (1,)), ((), ()))
F32 = jnp.float32
BF16 = jnp.bfloat16
PANEL = 32
TOP = 230.0


def encode(value, code_ref, peak_ref, k):
    parts = [value[:, i:i + 128].reshape(R // 8, 8, 128) for i in range(0, PC, 128)]
    peak = jnp.maximum(jnp.max(jnp.abs(parts[0]), axis=0), 1e-30)
    for part in parts[1:]:
        peak = jnp.maximum(peak, jnp.max(jnp.abs(part), axis=0))
    peak_ref[k] = peak
    gain = TOP / peak
    for i, part in enumerate(parts):
        scaled = part * gain
        power = scaled * scaled
        power = power * power
        power = power * power
        power = power * power
        power = jnp.where(scaled < 0.0, -power, power)
        code_ref[k, :, i * 128:(i + 1) * 128] = power.reshape(R, 128).astype(BF16)


def decode(code_ref, peak_ref, k):
    gain = peak_ref[k] * (1.0 / TOP)
    out = []
    for i in range(0, PC, 128):
        power = code_ref[k, :, i:i + 128].astype(F32)
        root = lax.rsqrt(lax.rsqrt(lax.rsqrt(lax.rsqrt(jnp.abs(power)))))
        root = jnp.where(power < 0.0, -root, root).reshape(R // 8, 8, 128) * gain
        out.append(root.reshape(R, 128))
    return jnp.concatenate(out, axis=1)


def fused_kernel(scale, s_hbm, om_ref, core_ref, next_ref,
                 sv, sl, sr, rl, rr, slp, srp, rlp, rrp, held, y_ref, yown, yr, yl, yopp, cacc, gacc,
                 gp, gin, part, zin, gfull, cp, cin, csum, cz, m_ref, inv_ref,
                 load_sem, sls, srs, rls, rrs, slps, srps, rlps, rrps,
                 gsl, gsr, grr, grl, fsl, fsr, frr, frl,
                 near_sem, gss, grs, zss, zrs, ass, ars, css, crs, dss, drs):
    node = lax.axis_index("node")
    me = lax.axis_index("samp")
    z = node // 8
    v = lax.rem(node, 8)
    u = me * 8 + v
    left = lax.rem(me + 3, 4)
    right = lax.rem(me + 1, 4)
    opp = lax.rem(me + 2, 4)

    def ids(node_to, samp_to):
        return {"node": node_to, "samp": samp_to}

    def group_peer(i):
        w = lax.rem(u + i, 32)
        return w, ids(z * 8 + lax.rem(w, 8), w // 8)

    def z_peer(i):
        w = lax.rem(z + i, 8)
        return w, ids(w * 8 + v, me)

    def v_peer(i):
        w = lax.rem(v + i, 8)
        return w, ids(z * 8 + w, me)

    order = [(opp, 0), (opp, 2), (opp, 1), (opp, 3),
             (left, 2), (right, 0), (left, 3), (right, 1),
             (left, 0), (right, 2), (left, 1), (right, 3),
             (me, 0), (me, 2), (me, 1), (me, 3)]
    where = {"opp": [0, 2, 1, 3], "left": [8, 10, 4, 6], "right": [5, 7, 9, 11], "me": [12, 14, 13, 15]}
    loads = []
    for pos, (chunk, piece) in enumerate(order):
        start = pl.multiple_of(chunk * 2048 + piece * PC, PC)
        copy = pltpu.make_async_copy(s_hbm.at[pl.ds(start, PC), :], sv.at[pos], load_sem.at[pos])
        copy.start()
        loads.append(copy)

    barrier = pltpu.get_barrier_semaphore()

    y = v // 2
    near = [ids(node, left), ids(node, right),
            ids(z * 8 + y * 2 + 1 - lax.rem(v, 2), me),
            ids(z * 8 + lax.rem(v + 2, 8), me), ids(z * 8 + lax.rem(v + 6, 8), me),
            ids(lax.rem(node + 8, 64), me), ids(lax.rem(node + 56, 64), me)]

    def greet(semaphore):
        for device in near:
            pl.semaphore_signal(semaphore, inc=1, device_id=device, device_id_type=MESH)

    def widen(i):
        pl.semaphore_wait(near_sem.at[i], 7)
        if i + 1 < 5:
            greet(near_sem.at[i + 1])

    greet(barrier)
    source_x = z // 2

    def sketch(pos):
        loads[pos].wait()
        return lax.dot_general(om_ref[...], sv[pos], NT, preferred_element_type=F32)

    def remote(src, dst, ssem, rsem, device):
        return pltpu.make_async_remote_copy(src_ref=src, dst_ref=dst, send_sem=ssem, recv_sem=rsem,
                                            device_id=device, device_id_type=MESH)

    def send(src, dst, ssem, rsem, peer):
        copy = remote(src, dst, ssem, rsem, {"samp": peer})
        copy.start()
        return copy

    to_left = [None] * 6
    to_right = [None] * 6

    def send_left(k):
        to_left[k] = (send(sl.at[k], rr.at[k], sls.at[k], rrs.at[k], left),
                      send(slp.at[k], rrp.at[k], slps.at[k], rrps.at[k], left))

    def send_right(k):
        to_right[k] = (send(sr.at[k], rl.at[k], srs.at[k], rls.at[k], right),
                       send(srp.at[k], rlp.at[k], srps.at[k], rlps.at[k], right))

    def from_right(k):
        for copy in to_left[k]:
            copy.wait_recv()
        return decode(rr, rrp, k)

    def from_left(k):
        for copy in to_right[k]:
            copy.wait_recv()
        return decode(rl, rlp, k)

    encode(sketch(0), sl, slp, 0)
    encode(sketch(1), sr, srp, 0)

    pl.semaphore_wait(barrier, 7)
    send_left(0)
    send_right(0)
    greet(near_sem.at[0])
    for k, (a, b) in enumerate([(2, 3), (4, 5), (6, 7)]):
        encode(sketch(a), sl, slp, k + 1)
        send_left(k + 1)
        encode(sketch(b), sr, srp, k + 1)
        send_right(k + 1)
        widen(k)
    for k in range(2):
        held[2 * k] = sketch(8 + 2 * k)
        held[2 * k + 1] = sketch(9 + 2 * k)
    widen(3)
    for pos, piece in ((12, 0), (13, 2), (14, 1), (15, 3)):
        y_ref[:, piece * PC:(piece + 1) * PC] = sketch(pos)
    widen(4)

    for k in range(2):
        encode(held[2 * k] + from_right(k), sl, slp, 4 + k)
        send_left(4 + k)
        encode(held[2 * k + 1] + from_left(k), sr, srp, 4 + k)
        send_right(4 + k)

    for k in range(2):
        y_ref[:, k * PC:(k + 1) * PC] += from_left(2 + k)
        y_ref[:, (2 + k) * PC:(3 + k) * PC] += from_right(2 + k)

    gather_left = [None] * 4
    gather_right = [None] * 4

    def finish(piece, last):
        columns = slice(piece * PC, (piece + 1) * PC)
        value = y_ref[:, columns] + last
        y_ref[:, columns] = value
        yown[piece] = value.astype(BF16)
        gram = lax.dot_general(value, value, NT, precision=HIGH, preferred_element_type=F32)
        if piece == 0:
            gacc[...] = gram
        else:
            gacc[...] += gram

    def gather(piece):
        gather_left[piece] = send(yown.at[piece], yr.at[piece], gsl.at[piece], grr.at[piece], left)
        gather_right[piece] = send(yown.at[piece], yl.at[piece], gsr.at[piece], grl.at[piece], right)

    finish(0, from_right(4))
    gather(0)
    finish(2, from_left(4))
    finish(1, from_right(5))
    finish(3, from_left(5))

    gram = gacc[...]
    gp[0:20] = gram[:, 0:128].reshape(20, 8, 128)
    gp[20:32] = jnp.zeros((12, 8, 128), F32)
    gp[20:24, :, 0:32] = gram[128:160, 128:160].reshape(4, 8, 32)

    def gram_out(i, carry):
        w, device = group_peer(i)
        remote(gp.at[w], gin.at[u], gss.at[i], grs.at[i], device).start()
        return carry

    lax.fori_loop(1, 32, gram_out, 0)
    gather(2)
    gather(1)
    gather(3)
    gin[u] = gp[u]

    def coeff(rows, name, piece):
        return jnp.dot(rows, sv[where[name][piece]], preferred_element_type=F32)

    cacc[...] = coeff(yown[0], "me", 0)
    for piece in (2, 1, 3):
        cacc[...] += coeff(yown[piece], "me", piece)

    def gram_in(i, carry):
        remote(gp.at[0], gin.at[0], gss.at[i], grs.at[i], ids(node, me)).wait_recv()
        return carry

    lax.fori_loop(1, 32, gram_in, 0)
    total = gin[0]
    for w in range(1, 32):
        total = total + gin[w]
    part[...] = total
    z_sends = []
    for i in range(1, 8):
        w, device = z_peer(i)
        copy = remote(part, zin.at[z], zss.at[i], zrs.at[i], device)
        copy.start()
        z_sends.append(copy)
    zin[z] = total

    def sides(piece):
        gather_left[piece].wait_recv()
        cacc[...] += coeff(yr[piece], "right", piece)
        gather_right[piece].wait_recv()
        cacc[...] += coeff(yl[piece], "left", piece)

    sides(0)
    sides(2)

    for copy in z_sends:
        copy.wait_recv()
    total = zin[0]
    for w in range(1, 8):
        total = total + zin[w]
    gfull[u] = total

    def share(i, carry):
        w, device = group_peer(i)
        remote(gfull.at[u], gfull.at[u], ass.at[i], ars.at[i], device).start()
        return carry

    lax.fori_loop(1, 32, share, 0)

    forward = [None] * 4

    def relay(piece):
        h = piece % 2
        if piece < 2:
            forward[piece] = send(yr.at[piece], yopp.at[piece], fsl.at[h], frr.at[h], left)
        else:
            forward[piece] = send(yl.at[piece], yopp.at[piece], fsr.at[h], frl.at[h], right)

    relay(0)
    relay(2)
    sides(1)
    relay(1)
    sides(3)
    relay(3)

    def shared_in(i, carry):
        remote(gfull.at[0], gfull.at[0], ass.at[i], ars.at[i], ids(node, me)).wait_recv()
        return carry

    lax.fori_loop(1, 32, shared_in, 0)

    lower = gfull[0:20].reshape(R, 128) * scale
    m_ref[:, 0:128] = lower
    m_ref[0:128, 128:160] = lower[128:160, :].T
    m_ref[128:160, 128:160] = gfull[20:24].reshape(32, 128)[:, 0:32] * scale
    lane = lax.broadcasted_iota(jnp.int32, (1, R), 1)
    lanes = lax.broadcasted_iota(jnp.int32, (PANEL, R), 1)
    row_id = lax.broadcasted_iota(jnp.int32, (PANEL, 1), 0)

    def panel(p):
        base = p * PANEL
        block = m_ref[base:base + PANEL, :]
        dinv = jnp.zeros((PANEL, 1), F32)
        for t in range(PANEL):
            k = base + t
            row = block[t:t + 1, :]
            inverse = 1.0 / block[t:t + 1, k:k + 1]
            dinv = jnp.where(row_id == t, inverse, dinv)
            if t + 1 < PANEL:
                col = jnp.where(row_id > t, block[:, k:k + 1] * inverse, 0.0)
                block = block - col * jnp.where(lane == k, row + 1.0, row)
        rows = lax.broadcasted_iota(jnp.int32, (PANEL, R), 0) + base
        unit = jnp.where(lanes < rows, block, jnp.where(lanes == rows, 1.0, 0.0))
        inv_ref[base:base + PANEL, :] = unit * jnp.sqrt(dinv)
        if base + PANEL < R:
            inside = (lanes >= base) & (lanes < base + PANEL)
            rest = jnp.where(inside, unit, block)
            update = lax.dot_general(block * dinv, rest, (((0,), (0,)), ((), ())),
                                     precision=HIGH, preferred_element_type=F32)
            below = slice(base + PANEL, R)
            keep = jnp.where((lane >= base) & (lane < base + PANEL), 0.0, m_ref[below, :])
            m_ref[below, :] = keep - update[below, :]

    panel(0)

    for piece in (0, 2, 1, 3):
        forward[piece].wait_recv()
        cacc[...] += coeff(yopp[piece], "opp", piece)
    top = cacc[0:128, :].T
    rest = cacc[128:160, :].T
    for w in range(8):
        for zl in range(2):
            start = (zl * 8 + w) * 32
            cp[w, zl * 32:(zl + 1) * 32, :] = top[start:start + 32, :]
            for h in range(2):
                g = zl * 2 + h
                cp[w, 64:80, g * 32:(g + 1) * 32] = rest[start + h * 16:start + h * 16 + 16, :]
    coeff_sends = []
    for i in range(1, 8):
        w, device = v_peer(i)
        copy = remote(cp.at[w], cin.at[v], css.at[i], crs.at[i], device)
        copy.start()
        coeff_sends.append(copy)
    cin[v] = cp[v]

    panel(1)
    panel(2)

    for copy in coeff_sends:
        copy.wait_recv()
    small = cin[0]
    for w in range(1, 8):
        small = small + cin[w]
    for t in range(8):
        g, h = t // 2, t % 2
        csum[t, :, 0:128] = small[t * 8:t * 8 + 8, :]
        csum[t, :, 128:160] = small[64 + h * 8:72 + h * 8, g * 32:(g + 1) * 32]

    def mine(t):
        return jnp.logical_and(2 * me + t // 4 == z, me == t % 4)

    for t in range(8):
        @pl.when(jnp.logical_not(mine(t)))
        def _():
            remote(csum.at[t], cz.at[z], dss.at[t], drs.at[z], ids((2 * me + t // 4) * 8 + v, t % 4)).start()

        @pl.when(mine(t))
        def _():
            cz[z] = csum[t]

    panel(3)
    panel(4)
    inv = inv_ref[...]
    core_ref[...] = jnp.dot(inv, y_ref[...], precision=HIGH, preferred_element_type=F32)

    for zs in range(8):
        @pl.when(jnp.logical_or(zs != z, source_x != me))
        def _():
            remote(csum.at[0], cz.at[zs], dss.at[0], drs.at[zs], ids(node, me)).wait_recv()
    out = cz[0]
    for w in range(1, 8):
        out = out + cz[w]
    next_ref[...] = lax.dot_general(out * scale, inv, NT, precision=HIGH, preferred_element_type=F32)

    def drain(i, carry):
        remote(gp.at[0], gin.at[0], gss.at[i], grs.at[i], ids(node, me)).wait_send()
        remote(gfull.at[0], gfull.at[0], ass.at[i], ars.at[i], ids(node, me)).wait_send()
        return carry

    lax.fori_loop(1, 32, drain, 0)
    for pair in to_left + to_right:
        pair[0].wait_send()
        pair[1].wait_send()
    for copy in gather_left + gather_right + forward + coeff_sends + z_sends:
        copy.wait_send()
    for t in range(8):
        @pl.when(jnp.logical_not(mine(t)))
        def _():
            remote(csum.at[t], cz.at[0], dss.at[t], drs.at[0], ids(node, me)).wait_send()


def body(snapshots, sketch_matrix):
    node_total = snapshots.shape[0] * lax.axis_size("node")
    vmem = pl.BlockSpec(memory_space=pltpu.VMEM)
    dma = pltpu.SemaphoreType.DMA
    shape = jax.ShapeDtypeStruct
    scratch = pltpu.VMEM
    core, nxt = pl.pallas_call(
        functools.partial(fused_kernel, 1.0 / node_total),
        out_shape=(shape((R, 2048), F32), shape((8, R), F32)),
        in_specs=[pl.BlockSpec(memory_space=pl.ANY), vmem],
        out_specs=(vmem, vmem),
        scratch_shapes=[
            scratch((16, PC, PC), BF16),
            scratch((6, R, PC), BF16), scratch((6, R, PC), BF16),
            scratch((6, R, PC), BF16), scratch((6, R, PC), BF16),
            scratch((6, 8, 128), F32), scratch((6, 8, 128), F32),
            scratch((6, 8, 128), F32), scratch((6, 8, 128), F32),
            scratch((4, R, PC), F32), scratch((R, 2048), F32),
            scratch((4, R, PC), BF16), scratch((4, R, PC), BF16),
            scratch((4, R, PC), BF16), scratch((4, R, PC), BF16),
            scratch((R, PC), F32), scratch((R, R), F32),
            scratch((32, 8, 128), F32), scratch((32, 8, 128), F32), scratch((8, 128), F32),
            scratch((8, 8, 128), F32), scratch((32, 8, 128), F32),
            scratch((8, 80, 128), F32), scratch((8, 80, 128), F32),
            scratch((8, 8, R), F32), scratch((8, 8, R), F32),
            scratch((R, R), F32), scratch((R, R), F32),
            dma((16,)), dma((6,)), dma((6,)), dma((6,)), dma((6,)),
            dma((6,)), dma((6,)), dma((6,)), dma((6,)),
            dma((4,)), dma((4,)), dma((4,)), dma((4,)),
            dma((2,)), dma((2,)), dma((2,)), dma((2,)),
            pltpu.SemaphoreType.REGULAR((5,)),
            dma((32,)), dma((32,)), dma((8,)), dma((8,)), dma((32,)), dma((32,)),
            dma((8,)), dma((8,)), dma((8,)), dma((8,)),
        ],
        compiler_params=pltpu.CompilerParams(collective_id=0, has_side_effects=True),
    )(snapshots, sketch_matrix.T)
    return core.T, nxt.T


def solution(mesh):
    placed = (P("node", "samp"), P("samp", None))
    return jax.shard_map(
        body,
        mesh=mesh,
        in_specs=placed,
        out_specs=(P(("node", "samp"), None), P("node", "samp")),
        check_vma=False,
    )
```

```python
import functools
import jax
import jax.numpy as jnp
from jax import lax
from jax.experimental import pallas as pl
from jax.experimental.pallas import tpu as pltpu
from jax.sharding import PartitionSpec as P

MESH = pl.DeviceIdType.MESH
HIGH = lax.Precision.HIGHEST
R = 160
PC = 512
NT = (((1,), (1,)), ((), ()))
F32 = jnp.float32
BF16 = jnp.bfloat16
PANEL = 40
TOP = 230.0


def encode(value, code_ref, peak_ref, k):
    parts = [value[:, i:i + 128].reshape(R // 8, 8, 128) for i in range(0, PC, 128)]
    peak = jnp.maximum(jnp.max(jnp.abs(parts[0]), axis=0), 1e-30)
    for part in parts[1:]:
        peak = jnp.maximum(peak, jnp.max(jnp.abs(part), axis=0))
    peak_ref[k] = peak
    gain = TOP / peak
    for i, part in enumerate(parts):
        scaled = part * gain
        power = scaled * scaled
        power = power * power
        power = power * power
        power = power * power
        power = jnp.where(scaled < 0.0, -power, power)
        code_ref[k, :, i * 128:(i + 1) * 128] = power.reshape(R, 128).astype(BF16)


def decode(code_ref, peak_ref, k):
    gain = peak_ref[k] * (1.0 / TOP)
    out = []
    for i in range(0, PC, 128):
        power = code_ref[k, :, i:i + 128].astype(F32)
        root = lax.rsqrt(lax.rsqrt(lax.rsqrt(lax.rsqrt(jnp.abs(power)))))
        root = jnp.where(power < 0.0, -root, root).reshape(R // 8, 8, 128) * gain
        out.append(root.reshape(R, 128))
    return jnp.concatenate(out, axis=1)


def fused_kernel(scale, s_hbm, om_ref, core_ref, next_ref,
                 sv, sl, sr, rl, rr, slp, srp, rlp, rrp, held, y_ref, yown, yr, yl, yopp, cacc, gacc,
                 gp, gin, part, zin, gfull, cp, cin, csum, cz, m_ref, inv_ref,
                 load_sem, sls, srs, rls, rrs, slps, srps, rlps, rrps,
                 gsl, gsr, grr, grl, fsl, fsr, frr, frl,
                 near_sem, gss, grs, zss, zrs, ass, ars, css, crs, dss, drs):
    node = lax.axis_index("node")
    me = lax.axis_index("samp")
    z = node // 8
    v = lax.rem(node, 8)
    u = me * 8 + v
    left = lax.rem(me + 3, 4)
    right = lax.rem(me + 1, 4)
    opp = lax.rem(me + 2, 4)

    def ids(node_to, samp_to):
        return {"node": node_to, "samp": samp_to}

    def group_peer(i):
        w = lax.rem(u + i, 32)
        return w, ids(z * 8 + lax.rem(w, 8), w // 8)

    def z_peer(i):
        w = lax.rem(z + i, 8)
        return w, ids(w * 8 + v, me)

    def v_peer(i):
        w = lax.rem(v + i, 8)
        return w, ids(z * 8 + w, me)

    order = [(opp, 0), (opp, 2), (opp, 1), (opp, 3),
             (left, 2), (right, 0), (left, 3), (right, 1),
             (left, 0), (right, 2), (left, 1), (right, 3),
             (me, 0), (me, 2), (me, 1), (me, 3)]
    where = {"opp": [0, 2, 1, 3], "left": [8, 10, 4, 6], "right": [5, 7, 9, 11], "me": [12, 14, 13, 15]}
    loads = []
    for pos, (chunk, piece) in enumerate(order):
        start = pl.multiple_of(chunk * 2048 + piece * PC, PC)
        copy = pltpu.make_async_copy(s_hbm.at[pl.ds(start, PC), :], sv.at[pos], load_sem.at[pos])
        copy.start()
        loads.append(copy)

    barrier = pltpu.get_barrier_semaphore()

    y = v // 2
    near = [ids(node, left), ids(node, right),
            ids(z * 8 + y * 2 + 1 - lax.rem(v, 2), me),
            ids(z * 8 + lax.rem(v + 2, 8), me), ids(z * 8 + lax.rem(v + 6, 8), me),
            ids(lax.rem(node + 8, 64), me), ids(lax.rem(node + 56, 64), me)]

    def greet(semaphore):
        for device in near:
            pl.semaphore_signal(semaphore, inc=1, device_id=device, device_id_type=MESH)

    def widen(i):
        pl.semaphore_wait(near_sem.at[i], 7)
        if i + 1 < 5:
            greet(near_sem.at[i + 1])

    greet(barrier)
    source_x = z // 2

    def sketch(pos):
        loads[pos].wait()
        return lax.dot_general(om_ref[...], sv[pos], NT, preferred_element_type=F32)

    def remote(src, dst, ssem, rsem, device):
        return pltpu.make_async_remote_copy(src_ref=src, dst_ref=dst, send_sem=ssem, recv_sem=rsem,
                                            device_id=device, device_id_type=MESH)

    def send(src, dst, ssem, rsem, peer):
        copy = remote(src, dst, ssem, rsem, {"samp": peer})
        copy.start()
        return copy

    to_left = [None] * 6
    to_right = [None] * 6

    def send_left(k):
        to_left[k] = (send(sl.at[k], rr.at[k], sls.at[k], rrs.at[k], left),
                      send(slp.at[k], rrp.at[k], slps.at[k], rrps.at[k], left))

    def send_right(k):
        to_right[k] = (send(sr.at[k], rl.at[k], srs.at[k], rls.at[k], right),
                       send(srp.at[k], rlp.at[k], srps.at[k], rlps.at[k], right))

    def from_right(k):
        for copy in to_left[k]:
            copy.wait_recv()
        return decode(rr, rrp, k)

    def from_left(k):
        for copy in to_right[k]:
            copy.wait_recv()
        return decode(rl, rlp, k)

    encode(sketch(0), sl, slp, 0)
    encode(sketch(1), sr, srp, 0)

    pl.semaphore_wait(barrier, 7)
    send_left(0)
    send_right(0)
    greet(near_sem.at[0])
    for k, (a, b) in enumerate([(2, 3), (4, 5), (6, 7)]):
        encode(sketch(a), sl, slp, k + 1)
        send_left(k + 1)
        encode(sketch(b), sr, srp, k + 1)
        send_right(k + 1)
        widen(k)
    for k in range(2):
        held[2 * k] = sketch(8 + 2 * k)
        held[2 * k + 1] = sketch(9 + 2 * k)
    widen(3)
    for pos, piece in ((12, 0), (13, 2), (14, 1), (15, 3)):
        y_ref[:, piece * PC:(piece + 1) * PC] = sketch(pos)
    widen(4)

    for k in range(2):
        encode(held[2 * k] + from_right(k), sl, slp, 4 + k)
        send_left(4 + k)
        encode(held[2 * k + 1] + from_left(k), sr, srp, 4 + k)
        send_right(4 + k)

    for k in range(2):
        y_ref[:, k * PC:(k + 1) * PC] += from_left(2 + k)
        y_ref[:, (2 + k) * PC:(3 + k) * PC] += from_right(2 + k)

    gather_left = [None] * 4
    gather_right = [None] * 4

    def finish(piece, last):
        columns = slice(piece * PC, (piece + 1) * PC)
        value = y_ref[:, columns] + last
        y_ref[:, columns] = value
        yown[piece] = value.astype(BF16)
        gram = lax.dot_general(value, value, NT, precision=HIGH, preferred_element_type=F32)
        if piece == 0:
            gacc[...] = gram
        else:
            gacc[...] += gram

    def gather(piece):
        gather_left[piece] = send(yown.at[piece], yr.at[piece], gsl.at[piece], grr.at[piece], left)
        gather_right[piece] = send(yown.at[piece], yl.at[piece], gsr.at[piece], grl.at[piece], right)

    finish(0, from_right(4))
    gather(0)
    finish(2, from_left(4))
    finish(1, from_right(5))
    finish(3, from_left(5))

    gram = gacc[...]
    gp[0:20] = gram[:, 0:128].reshape(20, 8, 128)
    gp[20:32] = jnp.zeros((12, 8, 128), F32)
    gp[20:24, :, 0:32] = gram[128:160, 128:160].reshape(4, 8, 32)

    def gram_out(i, carry):
        w, device = group_peer(i)
        remote(gp.at[w], gin.at[u], gss.at[i], grs.at[i], device).start()
        return carry

    lax.fori_loop(1, 32, gram_out, 0)
    gather(2)
    gather(1)
    gather(3)
    gin[u] = gp[u]

    def coeff(rows, name, piece):
        return jnp.dot(rows, sv[where[name][piece]], preferred_element_type=F32)

    cacc[...] = coeff(yown[0], "me", 0)
    for piece in (2, 1, 3):
        cacc[...] += coeff(yown[piece], "me", piece)

    def gram_in(i, carry):
        remote(gp.at[0], gin.at[0], gss.at[i], grs.at[i], ids(node, me)).wait_recv()
        return carry

    lax.fori_loop(1, 32, gram_in, 0)
    total = gin[0]
    for w in range(1, 32):
        total = total + gin[w]
    part[...] = total
    z_sends = []
    for i in range(1, 8):
        w, device = z_peer(i)
        copy = remote(part, zin.at[z], zss.at[i], zrs.at[i], device)
        copy.start()
        z_sends.append(copy)
    zin[z] = total

    def sides(piece):
        gather_left[piece].wait_recv()
        cacc[...] += coeff(yr[piece], "right", piece)
        gather_right[piece].wait_recv()
        cacc[...] += coeff(yl[piece], "left", piece)

    sides(0)
    sides(2)

    for copy in z_sends:
        copy.wait_recv()
    total = zin[0]
    for w in range(1, 8):
        total = total + zin[w]
    gfull[u] = total

    def share(i, carry):
        w, device = group_peer(i)
        remote(gfull.at[u], gfull.at[u], ass.at[i], ars.at[i], device).start()
        return carry

    lax.fori_loop(1, 32, share, 0)

    forward = [None] * 4

    def relay(piece):
        h = piece % 2
        if piece < 2:
            forward[piece] = send(yr.at[piece], yopp.at[piece], fsl.at[h], frr.at[h], left)
        else:
            forward[piece] = send(yl.at[piece], yopp.at[piece], fsr.at[h], frl.at[h], right)

    relay(0)
    relay(2)
    sides(1)
    relay(1)
    sides(3)
    relay(3)

    def shared_in(i, carry):
        remote(gfull.at[0], gfull.at[0], ass.at[i], ars.at[i], ids(node, me)).wait_recv()
        return carry

    lax.fori_loop(1, 32, shared_in, 0)

    lower = gfull[0:20].reshape(R, 128) * scale
    m_ref[:, 0:128] = lower
    m_ref[0:128, 128:160] = lower[128:160, :].T
    m_ref[128:160, 128:160] = gfull[20:24].reshape(32, 128)[:, 0:32] * scale
    lane = lax.broadcasted_iota(jnp.int32, (1, R), 1)
    lanes = lax.broadcasted_iota(jnp.int32, (PANEL, R), 1)
    row_id = lax.broadcasted_iota(jnp.int32, (PANEL, R), 0)

    whole = m_ref[...]
    square = lax.broadcasted_iota(jnp.int32, (R, R), 0) == lax.broadcasted_iota(jnp.int32, (R, R), 1)
    diagonal = jnp.where(square, whole, 0.0)
    fit = lax.rsqrt(jnp.sum(diagonal, axis=0, keepdims=True))
    m_ref[...] = whole * lax.rsqrt(jnp.sum(diagonal, axis=1, keepdims=True)) * fit

    def panel(p):
        base = p * PANEL
        block = m_ref[base:base + PANEL, :]
        dinv = jnp.zeros((PANEL, R), F32)
        for t in range(0, PANEL, 2):
            k = base + t
            c0 = jnp.broadcast_to(block[:, k:k + 1], (PANEL, R))
            c1 = jnp.broadcast_to(block[:, k + 1:k + 2], (PANEL, R))
            a, b, c = c0[t:t + 1, :], c0[t + 1:t + 2, :], c1[t + 1:t + 2, :]
            over = 1.0 / (a * c - b * b)
            first = 1.0 / a
            dinv = jnp.where(row_id == t, first, jnp.where(row_id == t + 1, a * over, dinv))
            row0, row1 = block[t:t + 1, :], block[t + 1:t + 2, :]
            row0 = jnp.where(lane == k, row0 + 1.0, row0)
            row1 = jnp.where(lane == k + 1, row1 + 1.0, row1)
            low = row_id > t + 1
            block = (block - jnp.where(low, c0, 0.0) * ((c * row0 - b * row1) * over)
                     - jnp.where(low, c1, 0.0) * ((a * row1 - b * row0) * over)
                     - jnp.where(row_id == t + 1, b * first * row0, 0.0))
        rows = row_id + base
        unit = jnp.where(lanes < rows, block, jnp.where(lanes == rows, 1.0, 0.0))
        inv_ref[base:base + PANEL, :] = unit * jnp.sqrt(dinv) * fit
        if base + PANEL < R:
            inside = (lanes >= base) & (lanes < base + PANEL)
            rest = jnp.where(inside, unit, block)
            update = lax.dot_general(block * dinv, rest, (((0,), (0,)), ((), ())),
                                     precision=HIGH, preferred_element_type=F32)
            below = slice(base + PANEL, R)
            keep = jnp.where((lane >= base) & (lane < base + PANEL), 0.0, m_ref[below, :])
            m_ref[below, :] = keep - update[below, :]

    panel(0)

    for piece in (0, 2, 1, 3):
        forward[piece].wait_recv()
        cacc[...] += coeff(yopp[piece], "opp", piece)
    top = cacc[0:128, :].T
    rest = cacc[128:160, :].T
    for w in range(8):
        for zl in range(2):
            start = (zl * 8 + w) * 32
            cp[w, zl * 32:(zl + 1) * 32, :] = top[start:start + 32, :]
            for h in range(2):
                g = zl * 2 + h
                cp[w, 64:80, g * 32:(g + 1) * 32] = rest[start + h * 16:start + h * 16 + 16, :]
    coeff_sends = []
    for i in range(1, 8):
        w, device = v_peer(i)
        copy = remote(cp.at[w], cin.at[v], css.at[i], crs.at[i], device)
        copy.start()
        coeff_sends.append(copy)
    cin[v] = cp[v]

    panel(1)
    panel(2)

    for copy in coeff_sends:
        copy.wait_recv()
    small = cin[0]
    for w in range(1, 8):
        small = small + cin[w]
    for t in range(8):
        g, h = t // 2, t % 2
        csum[t, :, 0:128] = small[t * 8:t * 8 + 8, :]
        csum[t, :, 128:160] = small[64 + h * 8:72 + h * 8, g * 32:(g + 1) * 32]

    def mine(t):
        return jnp.logical_and(2 * me + t // 4 == z, me == t % 4)

    for t in range(8):
        @pl.when(jnp.logical_not(mine(t)))
        def _():
            remote(csum.at[t], cz.at[z], dss.at[t], drs.at[z], ids((2 * me + t // 4) * 8 + v, t % 4)).start()

        @pl.when(mine(t))
        def _():
            cz[z] = csum[t]

    panel(3)
    inv = inv_ref[...]
    core_ref[...] = jnp.dot(inv, y_ref[...], precision=HIGH, preferred_element_type=F32)

    for zs in range(8):
        @pl.when(jnp.logical_or(zs != z, source_x != me))
        def _():
            remote(csum.at[0], cz.at[zs], dss.at[0], drs.at[zs], ids(node, me)).wait_recv()
    out = cz[0]
    for w in range(1, 8):
        out = out + cz[w]
    next_ref[...] = lax.dot_general(out * scale, inv, NT, precision=HIGH, preferred_element_type=F32)

    def drain(i, carry):
        remote(gp.at[0], gin.at[0], gss.at[i], grs.at[i], ids(node, me)).wait_send()
        remote(gfull.at[0], gfull.at[0], ass.at[i], ars.at[i], ids(node, me)).wait_send()
        return carry

    lax.fori_loop(1, 32, drain, 0)
    for pair in to_left + to_right:
        pair[0].wait_send()
        pair[1].wait_send()
    for copy in gather_left + gather_right + forward + coeff_sends + z_sends:
        copy.wait_send()
    for t in range(8):
        @pl.when(jnp.logical_not(mine(t)))
        def _():
            remote(csum.at[t], cz.at[0], dss.at[t], drs.at[0], ids(node, me)).wait_send()


def body(snapshots, sketch_matrix):
    node_total = snapshots.shape[0] * lax.axis_size("node")
    vmem = pl.BlockSpec(memory_space=pltpu.VMEM)
    dma = pltpu.SemaphoreType.DMA
    shape = jax.ShapeDtypeStruct
    scratch = pltpu.VMEM
    core, nxt = pl.pallas_call(
        functools.partial(fused_kernel, 1.0 / node_total),
        out_shape=(shape((R, 2048), F32), shape((8, R), F32)),
        in_specs=[pl.BlockSpec(memory_space=pltpu.HBM), vmem],
        out_specs=(vmem, vmem),
        scratch_shapes=[
            scratch((16, PC, PC), BF16),
            scratch((6, R, PC), BF16), scratch((6, R, PC), BF16),
            scratch((6, R, PC), BF16), scratch((6, R, PC), BF16),
            scratch((6, 8, 128), F32), scratch((6, 8, 128), F32),
            scratch((6, 8, 128), F32), scratch((6, 8, 128), F32),
            scratch((4, R, PC), F32), scratch((R, 2048), F32),
            scratch((4, R, PC), BF16), scratch((4, R, PC), BF16),
            scratch((4, R, PC), BF16), scratch((4, R, PC), BF16),
            scratch((R, PC), F32), scratch((R, R), F32),
            scratch((32, 8, 128), F32), scratch((32, 8, 128), F32), scratch((8, 128), F32),
            scratch((8, 8, 128), F32), scratch((32, 8, 128), F32),
            scratch((8, 80, 128), F32), scratch((8, 80, 128), F32),
            scratch((8, 8, R), F32), scratch((8, 8, R), F32),
            scratch((R, R), F32), scratch((R, R), F32),
            dma((16,)), dma((6,)), dma((6,)), dma((6,)), dma((6,)),
            dma((6,)), dma((6,)), dma((6,)), dma((6,)),
            dma((4,)), dma((4,)), dma((4,)), dma((4,)),
            dma((2,)), dma((2,)), dma((2,)), dma((2,)),
            pltpu.SemaphoreType.REGULAR((5,)),
            dma((32,)), dma((32,)), dma((8,)), dma((8,)), dma((32,)), dma((32,)),
            dma((8,)), dma((8,)), dma((8,)), dma((8,)),
        ],
        compiler_params=pltpu.CompilerParams(collective_id=0, has_side_effects=True),
    )(snapshots, sketch_matrix.T)
    return core.T, nxt.T


def solution(mesh):
    placed = (P("node", "samp"), P("samp", None))
    return jax.shard_map(
        body,
        mesh=mesh,
        in_specs=placed,
        out_specs=(P(("node", "samp"), None), P("node", "samp")),
        check_vma=False,
    )
```

```python
import functools
import jax
import jax.numpy as jnp
from jax import lax
from jax.experimental import pallas as pl
from jax.experimental.pallas import tpu as pltpu
from jax.sharding import PartitionSpec as P

MESH = pl.DeviceIdType.MESH
HIGH = lax.Precision.HIGHEST
R = 160
PC = 512
NT = (((1,), (1,)), ((), ()))
F32 = jnp.float32
BF16 = jnp.bfloat16
PANEL = 40
TOP = 230.0


def encode(value, code_ref, peak_ref, k):
    parts = [value[:, i:i + 128].reshape(R // 8, 8, 128) for i in range(0, PC, 128)]
    peak = jnp.maximum(jnp.max(jnp.abs(parts[0]), axis=0), 1e-30)
    for part in parts[1:]:
        peak = jnp.maximum(peak, jnp.max(jnp.abs(part), axis=0))
    peak_ref[k] = peak
    gain = TOP / peak
    for i, part in enumerate(parts):
        scaled = part * gain
        power = scaled * scaled
        power = power * power
        power = power * power
        power = power * power
        power = jnp.where(scaled < 0.0, -power, power)
        code_ref[k, :, i * 128:(i + 1) * 128] = power.reshape(R, 128).astype(BF16)


def decode(code_ref, peak_ref, k):
    gain = peak_ref[k] * (1.0 / TOP)
    out = []
    for i in range(0, PC, 128):
        power = code_ref[k, :, i:i + 128].astype(F32)
        root = lax.rsqrt(lax.rsqrt(lax.rsqrt(lax.rsqrt(jnp.abs(power)))))
        root = jnp.where(power < 0.0, -root, root).reshape(R // 8, 8, 128) * gain
        out.append(root.reshape(R, 128))
    return jnp.concatenate(out, axis=1)


def fused_kernel(scale, s_hbm, om_ref, core_ref, next_ref,
                 sv, sl, sr, rl, rr, slp, srp, rlp, rrp, held, y_ref, yown, yr, yl, yopp, cacc, gacc,
                 gp, gin, part, zin, gfull, cp, cin, csum, cz, m_ref, inv_ref,
                 load_sem, sls, srs, rls, rrs, slps, srps, rlps, rrps,
                 gsl, gsr, grr, grl, fsl, fsr, frr, frl,
                 near_sem, gss, grs, zss, zrs, ass, ars, css, crs, dss, drs):
    node = lax.axis_index("node")
    me = lax.axis_index("samp")
    z = node // 8
    v = lax.rem(node, 8)
    u = me * 8 + v
    left = lax.rem(me + 3, 4)
    right = lax.rem(me + 1, 4)
    opp = lax.rem(me + 2, 4)

    def ids(node_to, samp_to):
        return {"node": node_to, "samp": samp_to}

    def group_peer(i):
        w = lax.rem(u + i, 32)
        return w, ids(z * 8 + lax.rem(w, 8), w // 8)

    def z_peer(i):
        w = lax.rem(z + i, 8)
        return w, ids(w * 8 + v, me)

    def v_peer(i):
        w = lax.rem(v + i, 8)
        return w, ids(z * 8 + w, me)

    order = [(opp, 0), (opp, 2), (opp, 1), (opp, 3),
             (left, 2), (right, 0), (left, 3), (right, 1),
             (left, 0), (right, 2), (left, 1), (right, 3),
             (me, 0), (me, 2), (me, 1), (me, 3)]
    where = {"opp": [0, 2, 1, 3], "left": [8, 10, 4, 6], "right": [5, 7, 9, 11], "me": [12, 14, 13, 15]}
    loads = []
    for pos, (chunk, piece) in enumerate(order):
        start = pl.multiple_of(chunk * 2048 + piece * PC, PC)
        copy = pltpu.make_async_copy(s_hbm.at[pl.ds(start, PC), :], sv.at[pos], load_sem.at[pos])
        copy.start()
        loads.append(copy)

    barrier = pltpu.get_barrier_semaphore()

    y = v // 2
    near = [ids(node, left), ids(node, right),
            ids(z * 8 + y * 2 + 1 - lax.rem(v, 2), me),
            ids(z * 8 + lax.rem(v + 2, 8), me), ids(z * 8 + lax.rem(v + 6, 8), me),
            ids(lax.rem(node + 8, 64), me), ids(lax.rem(node + 56, 64), me)]

    def greet(semaphore):
        for device in near:
            pl.semaphore_signal(semaphore, inc=1, device_id=device, device_id_type=MESH)

    def widen(i):
        pl.semaphore_wait(near_sem.at[i], 7)
        if i + 1 < 5:
            greet(near_sem.at[i + 1])

    greet(barrier)
    source_x = z // 2

    def sketch(pos):
        loads[pos].wait()
        return lax.dot_general(om_ref[...], sv[pos], NT, preferred_element_type=F32)

    def remote(src, dst, ssem, rsem, device):
        return pltpu.make_async_remote_copy(src_ref=src, dst_ref=dst, send_sem=ssem, recv_sem=rsem,
                                            device_id=device, device_id_type=MESH)

    def send(src, dst, ssem, rsem, peer):
        copy = remote(src, dst, ssem, rsem, {"samp": peer})
        copy.start()
        return copy

    to_left = [None] * 6
    to_right = [None] * 6

    def send_left(k):
        to_left[k] = (send(sl.at[k], rr.at[k], sls.at[k], rrs.at[k], left),
                      send(slp.at[k], rrp.at[k], slps.at[k], rrps.at[k], left))

    def send_right(k):
        to_right[k] = (send(sr.at[k], rl.at[k], srs.at[k], rls.at[k], right),
                       send(srp.at[k], rlp.at[k], srps.at[k], rlps.at[k], right))

    def from_right(k):
        for copy in to_left[k]:
            copy.wait_recv()
        return decode(rr, rrp, k)

    def from_left(k):
        for copy in to_right[k]:
            copy.wait_recv()
        return decode(rl, rlp, k)

    encode(sketch(0), sl, slp, 0)
    encode(sketch(1), sr, srp, 0)

    pl.semaphore_wait(barrier, 7)
    send_left(0)
    send_right(0)
    greet(near_sem.at[0])
    for k, (a, b) in enumerate([(2, 3), (4, 5), (6, 7)]):
        encode(sketch(a), sl, slp, k + 1)
        send_left(k + 1)
        encode(sketch(b), sr, srp, k + 1)
        send_right(k + 1)
        widen(k)
    for k in range(2):
        held[2 * k] = sketch(8 + 2 * k)
        held[2 * k + 1] = sketch(9 + 2 * k)
    widen(3)
    for pos, piece in ((12, 0), (13, 2), (14, 1), (15, 3)):
        y_ref[:, piece * PC:(piece + 1) * PC] = sketch(pos)
    widen(4)

    for k in range(2):
        encode(held[2 * k] + from_right(k), sl, slp, 4 + k)
        send_left(4 + k)
        encode(held[2 * k + 1] + from_left(k), sr, srp, 4 + k)
        send_right(4 + k)

    for k in range(2):
        y_ref[:, k * PC:(k + 1) * PC] += from_left(2 + k)
        y_ref[:, (2 + k) * PC:(3 + k) * PC] += from_right(2 + k)

    gather_left = [None] * 4
    gather_right = [None] * 4

    def finish(piece, last):
        columns = slice(piece * PC, (piece + 1) * PC)
        value = y_ref[:, columns] + last
        y_ref[:, columns] = value
        yown[piece] = value.astype(BF16)
        gram = lax.dot_general(value, value, NT, precision=HIGH, preferred_element_type=F32)
        if piece == 0:
            gacc[...] = gram
        else:
            gacc[...] += gram

    def gather(piece):
        gather_left[piece] = send(yown.at[piece], yr.at[piece], gsl.at[piece], grr.at[piece], left)
        gather_right[piece] = send(yown.at[piece], yl.at[piece], gsr.at[piece], grl.at[piece], right)

    finish(0, from_right(4))
    gather(0)
    finish(2, from_left(4))
    gather(2)
    finish(1, from_right(5))
    finish(3, from_left(5))

    gram = gacc[...]
    gp[0:20] = gram[:, 0:128].reshape(20, 8, 128)
    gp[20:32] = jnp.zeros((12, 8, 128), F32)
    gp[20:24, :, 0:32] = gram[128:160, 128:160].reshape(4, 8, 32)

    def gram_out(i, carry):
        w, device = group_peer(i)
        remote(gp.at[w], gin.at[u], gss.at[i], grs.at[i], device).start()
        return carry

    lax.fori_loop(1, 32, gram_out, 0)
    gather(1)
    gather(3)
    gin[u] = gp[u]

    def coeff(rows, name, piece):
        return jnp.dot(rows, sv[where[name][piece]], preferred_element_type=F32)

    cacc[...] = coeff(yown[0], "me", 0)
    for piece in (2, 1, 3):
        cacc[...] += coeff(yown[piece], "me", piece)

    def gram_in(i, carry):
        remote(gp.at[0], gin.at[0], gss.at[i], grs.at[i], ids(node, me)).wait_recv()
        return carry

    lax.fori_loop(1, 32, gram_in, 0)
    total = gin[0]
    for w in range(1, 32):
        total = total + gin[w]
    part[...] = total
    z_sends = []
    for i in range(1, 8):
        w, device = z_peer(i)
        copy = remote(part, zin.at[z], zss.at[i], zrs.at[i], device)
        copy.start()
        z_sends.append(copy)
    zin[z] = total

    def sides(piece):
        gather_left[piece].wait_recv()
        cacc[...] += coeff(yr[piece], "right", piece)
        gather_right[piece].wait_recv()
        cacc[...] += coeff(yl[piece], "left", piece)

    forward = [None] * 4

    def relay(piece):
        h = piece % 2
        if piece < 2:
            forward[piece] = send(yr.at[piece], yopp.at[piece], fsl.at[h], frr.at[h], left)
        else:
            forward[piece] = send(yl.at[piece], yopp.at[piece], fsr.at[h], frl.at[h], right)

    sides(0)
    relay(0)
    sides(2)
    relay(2)

    for copy in z_sends:
        copy.wait_recv()
    total = zin[0]
    for w in range(1, 8):
        total = total + zin[w]
    gfull[u] = total

    def share(i, carry):
        w, device = group_peer(i)
        remote(gfull.at[u], gfull.at[u], ass.at[i], ars.at[i], device).start()
        return carry

    lax.fori_loop(1, 32, share, 0)

    sides(1)
    relay(1)
    sides(3)
    relay(3)

    for piece in (0, 2, 1, 3):
        forward[piece].wait_recv()
        cacc[...] += coeff(yopp[piece], "opp", piece)
    top = cacc[0:128, :].T
    rest = cacc[128:160, :].T
    for w in range(8):
        for zl in range(2):
            start = (zl * 8 + w) * 32
            cp[w, zl * 32:(zl + 1) * 32, :] = top[start:start + 32, :]
            for h in range(2):
                g = zl * 2 + h
                cp[w, 64:80, g * 32:(g + 1) * 32] = rest[start + h * 16:start + h * 16 + 16, :]
    coeff_sends = []
    for i in range(1, 8):
        w, device = v_peer(i)
        copy = remote(cp.at[w], cin.at[v], css.at[i], crs.at[i], device)
        copy.start()
        coeff_sends.append(copy)
    cin[v] = cp[v]

    def shared_in(i, carry):
        remote(gfull.at[0], gfull.at[0], ass.at[i], ars.at[i], ids(node, me)).wait_recv()
        return carry

    lax.fori_loop(1, 32, shared_in, 0)

    lower = gfull[0:20].reshape(R, 128) * scale
    m_ref[:, 0:128] = lower
    m_ref[0:128, 128:160] = lower[128:160, :].T
    m_ref[128:160, 128:160] = gfull[20:24].reshape(32, 128)[:, 0:32] * scale
    lane = lax.broadcasted_iota(jnp.int32, (1, R), 1)
    lanes = lax.broadcasted_iota(jnp.int32, (PANEL, R), 1)
    row_id = lax.broadcasted_iota(jnp.int32, (PANEL, R), 0)

    whole = m_ref[...]
    square = lax.broadcasted_iota(jnp.int32, (R, R), 0) == lax.broadcasted_iota(jnp.int32, (R, R), 1)
    diagonal = jnp.where(square, whole, 0.0)
    fit = lax.rsqrt(jnp.sum(diagonal, axis=0, keepdims=True))
    m_ref[...] = whole * lax.rsqrt(jnp.sum(diagonal, axis=1, keepdims=True)) * fit

    def panel(p):
        base = p * PANEL
        block = m_ref[base:base + PANEL, :]
        dinv = jnp.zeros((PANEL, R), F32)
        for t in range(0, PANEL, 2):
            k = base + t
            c0 = jnp.broadcast_to(block[:, k:k + 1], (PANEL, R))
            c1 = jnp.broadcast_to(block[:, k + 1:k + 2], (PANEL, R))
            a, b, c = c0[t:t + 1, :], c0[t + 1:t + 2, :], c1[t + 1:t + 2, :]
            over = 1.0 / (a * c - b * b)
            first = 1.0 / a
            dinv = jnp.where(row_id == t, first, jnp.where(row_id == t + 1, a * over, dinv))
            row0, row1 = block[t:t + 1, :], block[t + 1:t + 2, :]
            row0 = jnp.where(lane == k, row0 + 1.0, row0)
            row1 = jnp.where(lane == k + 1, row1 + 1.0, row1)
            low = row_id > t + 1
            block = (block - jnp.where(low, c0, 0.0) * ((c * row0 - b * row1) * over)
                     - jnp.where(low, c1, 0.0) * ((a * row1 - b * row0) * over)
                     - jnp.where(row_id == t + 1, b * first * row0, 0.0))
        rows = row_id + base
        unit = jnp.where(lanes < rows, block, jnp.where(lanes == rows, 1.0, 0.0))
        inv_ref[base:base + PANEL, :] = unit * jnp.sqrt(dinv) * fit
        if base + PANEL < R:
            inside = (lanes >= base) & (lanes < base + PANEL)
            rest = jnp.where(inside, unit, block)
            update = lax.dot_general(block * dinv, rest, (((0,), (0,)), ((), ())),
                                     precision=HIGH, preferred_element_type=F32)
            below = slice(base + PANEL, R)
            keep = jnp.where((lane >= base) & (lane < base + PANEL), 0.0, m_ref[below, :])
            m_ref[below, :] = keep - update[below, :]

    panel(0)

    panel(1)
    panel(2)

    for copy in coeff_sends:
        copy.wait_recv()
    small = cin[0]
    for w in range(1, 8):
        small = small + cin[w]
    for t in range(8):
        g, h = t // 2, t % 2
        csum[t, :, 0:128] = small[t * 8:t * 8 + 8, :]
        csum[t, :, 128:160] = small[64 + h * 8:72 + h * 8, g * 32:(g + 1) * 32]

    def mine(t):
        return jnp.logical_and(2 * me + t // 4 == z, me == t % 4)

    for t in range(8):
        @pl.when(jnp.logical_not(mine(t)))
        def _():
            remote(csum.at[t], cz.at[z], dss.at[t], drs.at[z], ids((2 * me + t // 4) * 8 + v, t % 4)).start()

        @pl.when(mine(t))
        def _():
            cz[z] = csum[t]

    panel(3)
    inv = inv_ref[...]
    core_ref[...] = jnp.dot(inv, y_ref[...], precision=HIGH, preferred_element_type=F32)

    for zs in range(8):
        @pl.when(jnp.logical_or(zs != z, source_x != me))
        def _():
            remote(csum.at[0], cz.at[zs], dss.at[0], drs.at[zs], ids(node, me)).wait_recv()
    out = cz[0]
    for w in range(1, 8):
        out = out + cz[w]
    next_ref[...] = lax.dot_general(out * scale, inv, NT, precision=HIGH, preferred_element_type=F32)

    def drain(i, carry):
        remote(gp.at[0], gin.at[0], gss.at[i], grs.at[i], ids(node, me)).wait_send()
        remote(gfull.at[0], gfull.at[0], ass.at[i], ars.at[i], ids(node, me)).wait_send()
        return carry

    lax.fori_loop(1, 32, drain, 0)
    for pair in to_left + to_right:
        pair[0].wait_send()
        pair[1].wait_send()
    for copy in gather_left + gather_right + forward + coeff_sends + z_sends:
        copy.wait_send()
    for t in range(8):
        @pl.when(jnp.logical_not(mine(t)))
        def _():
            remote(csum.at[t], cz.at[0], dss.at[t], drs.at[0], ids(node, me)).wait_send()


def body(snapshots, sketch_matrix):
    node_total = snapshots.shape[0] * lax.axis_size("node")
    vmem = pl.BlockSpec(memory_space=pltpu.VMEM)
    dma = pltpu.SemaphoreType.DMA
    shape = jax.ShapeDtypeStruct
    scratch = pltpu.VMEM
    core, nxt = pl.pallas_call(
        functools.partial(fused_kernel, 1.0 / node_total),
        out_shape=(shape((R, 2048), F32), shape((8, R), F32)),
        in_specs=[pl.BlockSpec(memory_space=pltpu.HBM), vmem],
        out_specs=(vmem, vmem),
        scratch_shapes=[
            scratch((16, PC, PC), BF16),
            scratch((6, R, PC), BF16), scratch((6, R, PC), BF16),
            scratch((6, R, PC), BF16), scratch((6, R, PC), BF16),
            scratch((6, 8, 128), F32), scratch((6, 8, 128), F32),
            scratch((6, 8, 128), F32), scratch((6, 8, 128), F32),
            scratch((4, R, PC), F32), scratch((R, 2048), F32),
            scratch((4, R, PC), BF16), scratch((4, R, PC), BF16),
            scratch((4, R, PC), BF16), scratch((4, R, PC), BF16),
            scratch((R, PC), F32), scratch((R, R), F32),
            scratch((32, 8, 128), F32), scratch((32, 8, 128), F32), scratch((8, 128), F32),
            scratch((8, 8, 128), F32), scratch((32, 8, 128), F32),
            scratch((8, 80, 128), F32), scratch((8, 80, 128), F32),
            scratch((8, 8, R), F32), scratch((8, 8, R), F32),
            scratch((R, R), F32), scratch((R, R), F32),
            dma((16,)), dma((6,)), dma((6,)), dma((6,)), dma((6,)),
            dma((6,)), dma((6,)), dma((6,)), dma((6,)),
            dma((4,)), dma((4,)), dma((4,)), dma((4,)),
            dma((2,)), dma((2,)), dma((2,)), dma((2,)),
            pltpu.SemaphoreType.REGULAR((5,)),
            dma((32,)), dma((32,)), dma((8,)), dma((8,)), dma((32,)), dma((32,)),
            dma((8,)), dma((8,)), dma((8,)), dma((8,)),
        ],
        compiler_params=pltpu.CompilerParams(collective_id=0, has_side_effects=True, vmem_limit_bytes=50 << 20),
    )(snapshots, sketch_matrix.T)
    return core.T, nxt.T


def solution(mesh):
    placed = (P("node", "samp"), P("samp", None))
    return jax.shard_map(
        body,
        mesh=mesh,
        in_specs=placed,
        out_specs=(P(("node", "samp"), None), P("node", "samp")),
        check_vma=False,
    )
```

```python
import functools
import jax
import jax.numpy as jnp
from jax import lax
from jax.experimental import pallas as pl
from jax.experimental.pallas import tpu as pltpu
from jax.sharding import PartitionSpec as P

MESH = pl.DeviceIdType.MESH
HIGH = lax.Precision.HIGHEST
R = 160
PC = 512
NT = (((1,), (1,)), ((), ()))
F32 = jnp.float32
BF16 = jnp.bfloat16
PANEL = 40
TOP = 230.0


def encode(value, code_ref, peak_ref, k):
    parts = [value[:, i:i + 128].reshape(R // 8, 8, 128) for i in range(0, PC, 128)]
    peak = jnp.maximum(jnp.max(jnp.abs(parts[0]), axis=0), 1e-30)
    for part in parts[1:]:
        peak = jnp.maximum(peak, jnp.max(jnp.abs(part), axis=0))
    peak_ref[k] = peak
    gain = TOP / peak
    for i, part in enumerate(parts):
        scaled = part * gain
        power = scaled * scaled
        power = power * power
        power = power * power
        power = power * power
        power = jnp.where(scaled < 0.0, -power, power)
        code_ref[k, :, i * 128:(i + 1) * 128] = power.reshape(R, 128).astype(BF16)


def decode(code_ref, peak_ref, k):
    gain = peak_ref[k] * (1.0 / TOP)
    out = []
    for i in range(0, PC, 128):
        power = code_ref[k, :, i:i + 128].astype(F32)
        root = lax.rsqrt(lax.rsqrt(lax.rsqrt(lax.rsqrt(jnp.abs(power)))))
        root = jnp.where(power < 0.0, -root, root).reshape(R // 8, 8, 128) * gain
        out.append(root.reshape(R, 128))
    return jnp.concatenate(out, axis=1)


def fused_kernel(scale, s_hbm, om_ref, core_ref, next_ref,
                 sv, sl, sr, rl, rr, slp, srp, rlp, rrp, held, y_ref, yown, yr, yl, yopp, cacc, gacc,
                 gp, gin, part, zin, gfull, cp, cin, csum, cz, m_ref, inv_ref,
                 load_sem, sls, srs, rls, rrs, slps, srps, rlps, rrps,
                 gsl, gsr, grr, grl, fsl, fsr, frr, frl,
                 near_sem, gss, grs, zss, zrs, ass, ars, css, crs, dss, drs):
    node = lax.axis_index("node")
    me = lax.axis_index("samp")
    z = node // 8
    v = lax.rem(node, 8)
    u = me * 8 + v
    left = lax.rem(me + 3, 4)
    right = lax.rem(me + 1, 4)
    opp = lax.rem(me + 2, 4)

    def ids(node_to, samp_to):
        return {"node": node_to, "samp": samp_to}

    def group_peer(i):
        w = lax.rem(u + i, 32)
        return w, ids(z * 8 + lax.rem(w, 8), w // 8)

    def z_peer(i):
        w = lax.rem(z + i, 8)
        return w, ids(w * 8 + v, me)

    def v_peer(i):
        w = lax.rem(v + i, 8)
        return w, ids(z * 8 + w, me)

    order = [(opp, 0), (opp, 2), (opp, 1), (opp, 3),
             (left, 2), (right, 0), (left, 3), (right, 1),
             (left, 0), (right, 2), (left, 1), (right, 3),
             (me, 0), (me, 2), (me, 1), (me, 3)]
    where = {"opp": [0, 2, 1, 3], "left": [8, 10, 4, 6], "right": [5, 7, 9, 11], "me": [12, 14, 13, 15]}
    loads = []
    for pos, (chunk, piece) in enumerate(order):
        start = pl.multiple_of(chunk * 2048 + piece * PC, PC)
        copy = pltpu.make_async_copy(s_hbm.at[pl.ds(start, PC), :], sv.at[pos], load_sem.at[pos])
        copy.start()
        loads.append(copy)

    barrier = pltpu.get_barrier_semaphore()

    y = v // 2
    near = [ids(node, left), ids(node, right),
            ids(z * 8 + y * 2 + 1 - lax.rem(v, 2), me),
            ids(z * 8 + lax.rem(v + 2, 8), me), ids(z * 8 + lax.rem(v + 6, 8), me),
            ids(lax.rem(node + 8, 64), me), ids(lax.rem(node + 56, 64), me)]

    def greet(semaphore):
        for device in near:
            pl.semaphore_signal(semaphore, inc=1, device_id=device, device_id_type=MESH)

    def widen(i):
        pl.semaphore_wait(near_sem.at[i], 7)
        if i + 1 < 5:
            greet(near_sem.at[i + 1])

    greet(barrier)
    source_x = z // 2

    def sketch(pos):
        loads[pos].wait()
        return lax.dot_general(om_ref[...], sv[pos], NT, preferred_element_type=F32)

    def remote(src, dst, ssem, rsem, device):
        return pltpu.make_async_remote_copy(src_ref=src, dst_ref=dst, send_sem=ssem, recv_sem=rsem,
                                            device_id=device, device_id_type=MESH)

    def send(src, dst, ssem, rsem, peer):
        copy = remote(src, dst, ssem, rsem, {"samp": peer})
        copy.start()
        return copy

    to_left = [None] * 6
    to_right = [None] * 6

    def send_left(k):
        to_left[k] = (send(sl.at[k], rr.at[k], sls.at[k], rrs.at[k], left),
                      send(slp.at[k], rrp.at[k], slps.at[k], rrps.at[k], left))

    def send_right(k):
        to_right[k] = (send(sr.at[k], rl.at[k], srs.at[k], rls.at[k], right),
                       send(srp.at[k], rlp.at[k], srps.at[k], rlps.at[k], right))

    def from_right(k):
        for copy in to_left[k]:
            copy.wait_recv()
        return decode(rr, rrp, k)

    def from_left(k):
        for copy in to_right[k]:
            copy.wait_recv()
        return decode(rl, rlp, k)

    encode(sketch(0), sl, slp, 0)
    encode(sketch(1), sr, srp, 0)

    pl.semaphore_wait(barrier, 7)
    send_left(0)
    send_right(0)
    greet(near_sem.at[0])
    for k, (a, b) in enumerate([(2, 3), (4, 5), (6, 7)]):
        encode(sketch(a), sl, slp, k + 1)
        send_left(k + 1)
        encode(sketch(b), sr, srp, k + 1)
        send_right(k + 1)
        widen(k)
    for k in range(2):
        held[2 * k] = sketch(8 + 2 * k)
        held[2 * k + 1] = sketch(9 + 2 * k)
    widen(3)
    for pos, piece in ((12, 0), (13, 2), (14, 1), (15, 3)):
        y_ref[:, piece * PC:(piece + 1) * PC] = sketch(pos)
    widen(4)

    for k in range(2):
        encode(held[2 * k] + from_right(k), sl, slp, 4 + k)
        send_left(4 + k)
        encode(held[2 * k + 1] + from_left(k), sr, srp, 4 + k)
        send_right(4 + k)

    for k in range(2):
        y_ref[:, k * PC:(k + 1) * PC] += from_left(2 + k)
        y_ref[:, (2 + k) * PC:(3 + k) * PC] += from_right(2 + k)

    gather_left = [None] * 4
    gather_right = [None] * 4

    def finish(piece, last):
        columns = slice(piece * PC, (piece + 1) * PC)
        value = y_ref[:, columns] + last
        y_ref[:, columns] = value
        yown[piece] = value.astype(BF16)
        gram = lax.dot_general(value, value, NT, precision=HIGH, preferred_element_type=F32)
        if piece == 0:
            gacc[...] = gram
        else:
            gacc[...] += gram

    def gather(piece):
        gather_left[piece] = send(yown.at[piece], yr.at[piece], gsl.at[piece], grr.at[piece], left)
        gather_right[piece] = send(yown.at[piece], yl.at[piece], gsr.at[piece], grl.at[piece], right)

    finish(0, from_right(4))
    gather(0)
    finish(2, from_left(4))
    gather(2)
    finish(1, from_right(5))
    finish(3, from_left(5))

    gram = gacc[...]
    gp[0:20] = gram[:, 0:128].reshape(20, 8, 128)
    gp[20:32] = jnp.zeros((12, 8, 128), F32)
    gp[20:24, :, 0:32] = gram[128:160, 128:160].reshape(4, 8, 32)

    def gram_out(i, carry):
        w, device = group_peer(i)
        remote(gp.at[w], gin.at[u], gss.at[i], grs.at[i], device).start()
        return carry

    lax.fori_loop(1, 32, gram_out, 0)
    gather(1)
    gather(3)
    gin[u] = gp[u]

    def coeff(rows, name, piece):
        return jnp.dot(rows, sv[where[name][piece]], preferred_element_type=F32)

    cacc[...] = coeff(yown[0], "me", 0)
    for piece in (2, 1, 3):
        cacc[...] += coeff(yown[piece], "me", piece)

    def gram_in(i, carry):
        remote(gp.at[0], gin.at[0], gss.at[i], grs.at[i], ids(node, me)).wait_recv()
        return carry

    lax.fori_loop(1, 32, gram_in, 0)
    total = gin[0]
    for w in range(1, 32):
        total = total + gin[w]
    part[...] = total
    z_sends = []
    for i in range(1, 8):
        w, device = z_peer(i)
        copy = remote(part, zin.at[z], zss.at[i], zrs.at[i], device)
        copy.start()
        z_sends.append(copy)
    zin[z] = total

    def sides(piece):
        gather_left[piece].wait_recv()
        cacc[...] += coeff(yr[piece], "right", piece)
        gather_right[piece].wait_recv()
        cacc[...] += coeff(yl[piece], "left", piece)

    forward = [None] * 4

    def relay(piece):
        h = piece % 2
        if piece < 2:
            forward[piece] = send(yr.at[piece], yopp.at[piece], fsl.at[h], frr.at[h], left)
        else:
            forward[piece] = send(yl.at[piece], yopp.at[piece], fsr.at[h], frl.at[h], right)

    sides(0)
    relay(0)
    sides(2)
    relay(2)

    for copy in z_sends:
        copy.wait_recv()
    total = zin[0]
    for w in range(1, 8):
        total = total + zin[w]
    gfull[u] = total

    def share(i, carry):
        w, device = group_peer(i)
        remote(gfull.at[u], gfull.at[u], ass.at[i], ars.at[i], device).start()
        return carry

    lax.fori_loop(1, 32, share, 0)

    sides(1)
    relay(1)
    sides(3)
    relay(3)

    for piece in (0, 2, 1, 3):
        forward[piece].wait_recv()
        cacc[...] += coeff(yopp[piece], "opp", piece)
    top = cacc[0:128, :].T
    rest = cacc[128:160, :].T
    for w in range(8):
        for zl in range(2):
            start = (zl * 8 + w) * 32
            cp[w, zl * 32:(zl + 1) * 32, :] = top[start:start + 32, :]
            for h in range(2):
                g = zl * 2 + h
                cp[w, 64:80, g * 32:(g + 1) * 32] = rest[start + h * 16:start + h * 16 + 16, :]
    coeff_sends = []
    for i in (4, 3, 5, 2, 6, 1, 7):
        w, device = v_peer(i)
        copy = remote(cp.at[w], cin.at[v], css.at[i], crs.at[i], device)
        copy.start()
        coeff_sends.append(copy)
    cin[v] = cp[v]

    def shared_in(i, carry):
        remote(gfull.at[0], gfull.at[0], ass.at[i], ars.at[i], ids(node, me)).wait_recv()
        return carry

    lax.fori_loop(1, 32, shared_in, 0)

    lower = gfull[0:20].reshape(R, 128) * scale
    m_ref[:, 0:128] = lower
    m_ref[0:128, 128:160] = lower[128:160, :].T
    m_ref[128:160, 128:160] = gfull[20:24].reshape(32, 128)[:, 0:32] * scale
    lane = lax.broadcasted_iota(jnp.int32, (1, R), 1)
    lanes = lax.broadcasted_iota(jnp.int32, (PANEL, R), 1)
    row_id = lax.broadcasted_iota(jnp.int32, (PANEL, R), 0)

    whole = m_ref[...]
    square = lax.broadcasted_iota(jnp.int32, (R, R), 0) == lax.broadcasted_iota(jnp.int32, (R, R), 1)
    diagonal = jnp.where(square, whole, 0.0)
    fit = lax.rsqrt(jnp.sum(diagonal, axis=0, keepdims=True))
    m_ref[...] = whole * lax.rsqrt(jnp.sum(diagonal, axis=1, keepdims=True)) * fit

    def panel(p):
        base = p * PANEL
        block = m_ref[base:base + PANEL, :]
        dinv = jnp.zeros((PANEL, R), F32)
        for t in range(0, PANEL, 2):
            k = base + t
            c0 = jnp.broadcast_to(block[:, k:k + 1], (PANEL, R))
            c1 = jnp.broadcast_to(block[:, k + 1:k + 2], (PANEL, R))
            a, b, c = c0[t:t + 1, :], c0[t + 1:t + 2, :], c1[t + 1:t + 2, :]
            over = 1.0 / (a * c - b * b)
            first = 1.0 / a
            dinv = jnp.where(row_id == t, first, jnp.where(row_id == t + 1, a * over, dinv))
            row0, row1 = block[t:t + 1, :], block[t + 1:t + 2, :]
            row0 = jnp.where(lane == k, row0 + 1.0, row0)
            row1 = jnp.where(lane == k + 1, row1 + 1.0, row1)
            low = row_id > t + 1
            block = (block - jnp.where(low, c0, 0.0) * ((c * row0 - b * row1) * over)
                     - jnp.where(low, c1, 0.0) * ((a * row1 - b * row0) * over)
                     - jnp.where(row_id == t + 1, b * first * row0, 0.0))
        rows = row_id + base
        unit = jnp.where(lanes < rows, block, jnp.where(lanes == rows, 1.0, 0.0))
        inv_ref[base:base + PANEL, :] = unit * jnp.sqrt(dinv) * fit
        if base + PANEL < R:
            inside = (lanes >= base) & (lanes < base + PANEL)
            rest = jnp.where(inside, unit, block)
            update = lax.dot_general(block * dinv, rest, (((0,), (0,)), ((), ())),
                                     precision=HIGH, preferred_element_type=F32)
            below = slice(base + PANEL, R)
            keep = jnp.where((lane >= base) & (lane < base + PANEL), 0.0, m_ref[below, :])
            m_ref[below, :] = keep - update[below, :]

    panel(0)

    panel(1)

    for copy in coeff_sends:
        copy.wait_recv()
    small = cin[0]
    for w in range(1, 8):
        small = small + cin[w]
    for t in range(8):
        g, h = t // 2, t % 2
        csum[t, :, 0:128] = small[t * 8:t * 8 + 8, :]
        csum[t, :, 128:160] = small[64 + h * 8:72 + h * 8, g * 32:(g + 1) * 32]

    def mine(t):
        return jnp.logical_and(2 * me + t // 4 == z, me == t % 4)

    for t in range(8):
        @pl.when(jnp.logical_not(mine(t)))
        def _():
            remote(csum.at[t], cz.at[z], dss.at[t], drs.at[z], ids((2 * me + t // 4) * 8 + v, t % 4)).start()

        @pl.when(mine(t))
        def _():
            cz[z] = csum[t]

    panel(2)
    panel(3)
    inv = inv_ref[...]
    core_ref[...] = jnp.dot(inv, y_ref[...], precision=HIGH, preferred_element_type=F32)

    def drain(i, carry):
        remote(gp.at[0], gin.at[0], gss.at[i], grs.at[i], ids(node, me)).wait_send()
        remote(gfull.at[0], gfull.at[0], ass.at[i], ars.at[i], ids(node, me)).wait_send()
        return carry

    lax.fori_loop(1, 32, drain, 0)
    for pair in to_left + to_right:
        pair[0].wait_send()
        pair[1].wait_send()
    for copy in gather_left + gather_right + forward + coeff_sends + z_sends:
        copy.wait_send()
    for zs in range(8):
        @pl.when(jnp.logical_or(zs != z, source_x != me))
        def _():
            remote(csum.at[0], cz.at[zs], dss.at[0], drs.at[zs], ids(node, me)).wait_recv()
    out = cz[0]
    for w in range(1, 8):
        out = out + cz[w]
    next_ref[...] = lax.dot_general(out * scale, inv, NT, precision=HIGH, preferred_element_type=F32)

    for t in range(8):
        @pl.when(jnp.logical_not(mine(t)))
        def _():
            remote(csum.at[t], cz.at[0], dss.at[t], drs.at[0], ids(node, me)).wait_send()


def body(snapshots, sketch_matrix):
    node_total = snapshots.shape[0] * lax.axis_size("node")
    vmem = pl.BlockSpec(memory_space=pltpu.VMEM)
    dma = pltpu.SemaphoreType.DMA
    shape = jax.ShapeDtypeStruct
    scratch = pltpu.VMEM
    core, nxt = pl.pallas_call(
        functools.partial(fused_kernel, 1.0 / node_total),
        out_shape=(shape((R, 2048), F32), shape((8, R), F32)),
        in_specs=[pl.BlockSpec(memory_space=pltpu.HBM), vmem],
        out_specs=(vmem, vmem),
        scratch_shapes=[
            scratch((16, PC, PC), BF16),
            scratch((6, R, PC), BF16), scratch((6, R, PC), BF16),
            scratch((6, R, PC), BF16), scratch((6, R, PC), BF16),
            scratch((6, 8, 128), F32), scratch((6, 8, 128), F32),
            scratch((6, 8, 128), F32), scratch((6, 8, 128), F32),
            scratch((4, R, PC), F32), scratch((R, 2048), F32),
            scratch((4, R, PC), BF16), scratch((4, R, PC), BF16),
            scratch((4, R, PC), BF16), scratch((4, R, PC), BF16),
            scratch((R, PC), F32), scratch((R, R), F32),
            scratch((32, 8, 128), F32), scratch((32, 8, 128), F32), scratch((8, 128), F32),
            scratch((8, 8, 128), F32), scratch((32, 8, 128), F32),
            scratch((8, 80, 128), F32), scratch((8, 80, 128), F32),
            scratch((8, 8, R), F32), scratch((8, 8, R), F32),
            scratch((R, R), F32), scratch((R, R), F32),
            dma((16,)), dma((6,)), dma((6,)), dma((6,)), dma((6,)),
            dma((6,)), dma((6,)), dma((6,)), dma((6,)),
            dma((4,)), dma((4,)), dma((4,)), dma((4,)),
            dma((2,)), dma((2,)), dma((2,)), dma((2,)),
            pltpu.SemaphoreType.REGULAR((5,)),
            dma((32,)), dma((32,)), dma((8,)), dma((8,)), dma((32,)), dma((32,)),
            dma((8,)), dma((8,)), dma((8,)), dma((8,)),
        ],
        compiler_params=pltpu.CompilerParams(collective_id=0, has_side_effects=True, vmem_limit_bytes=50 << 20),
    )(snapshots, sketch_matrix.T)
    return core.T, nxt.T


def solution(mesh):
    placed = (P("node", "samp"), P("samp", None))
    return jax.shard_map(
        body,
        mesh=mesh,
        in_specs=placed,
        out_specs=(P(("node", "samp"), None), P("node", "samp")),
        check_vma=False,
    )
```

```python
import functools
import jax
import jax.numpy as jnp
from jax import lax
from jax.experimental import pallas as pl
from jax.experimental.pallas import tpu as pltpu
from jax.sharding import PartitionSpec as P

MESH = pl.DeviceIdType.MESH
HIGH = lax.Precision.HIGHEST
R = 160
PC = 512
NT = (((1,), (1,)), ((), ()))
F32 = jnp.float32
BF16 = jnp.bfloat16
PANEL = 40
TOP = 230.0


def encode(value, code_ref, peak_ref, k):
    parts = [value[:, i:i + 128].reshape(R // 8, 8, 128) for i in range(0, PC, 128)]
    peak = jnp.maximum(jnp.max(jnp.abs(parts[0]), axis=0), 1e-30)
    for part in parts[1:]:
        peak = jnp.maximum(peak, jnp.max(jnp.abs(part), axis=0))
    peak_ref[k] = peak
    gain = TOP / peak
    for i, part in enumerate(parts):
        scaled = part * gain
        power = scaled * scaled
        power = power * power
        power = power * power
        power = power * power
        power = jnp.where(scaled < 0.0, -power, power)
        code_ref[k, :, i * 128:(i + 1) * 128] = power.reshape(R, 128).astype(BF16)


def decode(code_ref, peak_ref, k):
    gain = peak_ref[k] * (1.0 / TOP)
    out = []
    for i in range(0, PC, 128):
        power = code_ref[k, :, i:i + 128].astype(F32)
        root = lax.rsqrt(lax.rsqrt(lax.rsqrt(lax.rsqrt(jnp.abs(power)))))
        root = jnp.where(power < 0.0, -root, root).reshape(R // 8, 8, 128) * gain
        out.append(root.reshape(R, 128))
    return jnp.concatenate(out, axis=1)


def fused_kernel(scale, s_hbm, om_ref, core_ref, next_ref,
                 sv, sl, sr, rl, rr, slp, srp, rlp, rrp, held, y_ref, yown, yr, yl, yopp, cacc, gacc,
                 gp, gin, part, zin, part_x, xin, gfull, cp, cin, csum, cz, m_ref, inv_ref,
                 load_sem, sls, srs, rls, rrs, slps, srps, rlps, rrps,
                 gsl, gsr, grr, grl, fsl, fsr, frr, frl,
                 near_sem, gss, grs, zss, zrs, xss, xrs, ass, ars, css, crs, dss, drs):
    node = lax.axis_index("node")
    me = lax.axis_index("samp")
    z = node // 8
    v = lax.rem(node, 8)
    left = lax.rem(me + 3, 4)
    right = lax.rem(me + 1, 4)
    opp = lax.rem(me + 2, 4)

    def ids(node_to, samp_to):
        return {"node": node_to, "samp": samp_to}

    def z_peer(i):
        w = lax.rem(z + i, 8)
        return w, ids(w * 8 + v, me)

    def v_peer(i):
        w = lax.rem(v + i, 8)
        return w, ids(z * 8 + w, me)

    order = [(opp, 0), (opp, 2), (opp, 1), (opp, 3),
             (left, 2), (right, 0), (left, 3), (right, 1),
             (left, 0), (right, 2), (left, 1), (right, 3),
             (me, 0), (me, 2), (me, 1), (me, 3)]
    where = {"opp": [0, 2, 1, 3], "left": [8, 10, 4, 6], "right": [5, 7, 9, 11], "me": [12, 14, 13, 15]}
    loads = []
    for pos, (chunk, piece) in enumerate(order):
        start = pl.multiple_of(chunk * 2048 + piece * PC, PC)
        copy = pltpu.make_async_copy(s_hbm.at[pl.ds(start, PC), :], sv.at[pos], load_sem.at[pos])
        copy.start()
        loads.append(copy)

    barrier = pltpu.get_barrier_semaphore()

    y = v // 2
    near = [ids(node, left), ids(node, right),
            ids(z * 8 + y * 2 + 1 - lax.rem(v, 2), me),
            ids(z * 8 + lax.rem(v + 2, 8), me), ids(z * 8 + lax.rem(v + 6, 8), me),
            ids(lax.rem(node + 8, 64), me), ids(lax.rem(node + 56, 64), me)]

    def greet(semaphore):
        for device in near:
            pl.semaphore_signal(semaphore, inc=1, device_id=device, device_id_type=MESH)

    def widen(i):
        pl.semaphore_wait(near_sem.at[i], 7)
        if i + 1 < 5:
            greet(near_sem.at[i + 1])

    greet(barrier)
    source_x = z // 2

    def sketch(pos):
        loads[pos].wait()
        return lax.dot_general(om_ref[...], sv[pos], NT, preferred_element_type=F32)

    def remote(src, dst, ssem, rsem, device):
        return pltpu.make_async_remote_copy(src_ref=src, dst_ref=dst, send_sem=ssem, recv_sem=rsem,
                                            device_id=device, device_id_type=MESH)

    def send(src, dst, ssem, rsem, peer):
        copy = remote(src, dst, ssem, rsem, {"samp": peer})
        copy.start()
        return copy

    to_left = [None] * 6
    to_right = [None] * 6

    def send_left(k):
        to_left[k] = (send(sl.at[k], rr.at[k], sls.at[k], rrs.at[k], left),
                      send(slp.at[k], rrp.at[k], slps.at[k], rrps.at[k], left))

    def send_right(k):
        to_right[k] = (send(sr.at[k], rl.at[k], srs.at[k], rls.at[k], right),
                       send(srp.at[k], rlp.at[k], srps.at[k], rlps.at[k], right))

    def from_right(k):
        for copy in to_left[k]:
            copy.wait_recv()
        return decode(rr, rrp, k)

    def from_left(k):
        for copy in to_right[k]:
            copy.wait_recv()
        return decode(rl, rlp, k)

    encode(sketch(0), sl, slp, 0)
    encode(sketch(1), sr, srp, 0)

    pl.semaphore_wait(barrier, 7)
    send_left(0)
    send_right(0)
    greet(near_sem.at[0])
    for k, (a, b) in enumerate([(2, 3), (4, 5), (6, 7)]):
        encode(sketch(a), sl, slp, k + 1)
        send_left(k + 1)
        encode(sketch(b), sr, srp, k + 1)
        send_right(k + 1)
        widen(k)
    for k in range(2):
        held[2 * k] = sketch(8 + 2 * k)
        held[2 * k + 1] = sketch(9 + 2 * k)
    widen(3)
    for pos, piece in ((12, 0), (13, 2), (14, 1), (15, 3)):
        y_ref[:, piece * PC:(piece + 1) * PC] = sketch(pos)
    widen(4)

    for k in range(2):
        encode(held[2 * k] + from_right(k), sl, slp, 4 + k)
        send_left(4 + k)
        encode(held[2 * k + 1] + from_left(k), sr, srp, 4 + k)
        send_right(4 + k)

    for k in range(2):
        y_ref[:, k * PC:(k + 1) * PC] += from_left(2 + k)
        y_ref[:, (2 + k) * PC:(3 + k) * PC] += from_right(2 + k)

    gather_left = [None] * 4
    gather_right = [None] * 4

    def finish(piece, last):
        columns = slice(piece * PC, (piece + 1) * PC)
        value = y_ref[:, columns] + last
        y_ref[:, columns] = value
        yown[piece] = value.astype(BF16)
        gram = lax.dot_general(value, value, NT, precision=HIGH, preferred_element_type=F32)
        if piece == 0:
            gacc[...] = gram
        else:
            gacc[...] += gram

    def gather(piece):
        gather_left[piece] = send(yown.at[piece], yr.at[piece], gsl.at[piece], grr.at[piece], left)
        gather_right[piece] = send(yown.at[piece], yl.at[piece], gsr.at[piece], grl.at[piece], right)

    finish(0, from_right(4))
    gather(0)
    finish(2, from_left(4))
    gather(2)
    finish(1, from_right(5))
    finish(3, from_left(5))

    gram = gacc[...]
    gp[0:20] = gram[:, 0:128].reshape(20, 8, 128)
    gp[20:24] = jnp.zeros((4, 8, 128), F32)
    gp[20:24, :, 0:32] = gram[128:160, 128:160].reshape(4, 8, 32)

    gram_sends = []
    for i in range(1, 8):
        w, device = v_peer(i)
        copy = remote(gp.at[pl.ds(w * 3, 3)], gin.at[v], gss.at[i], grs.at[i], device)
        copy.start()
        gram_sends.append(copy)
    gather(1)
    gather(3)
    gin[v] = gp[pl.ds(v * 3, 3)]

    def coeff(rows, name, piece):
        return jnp.dot(rows, sv[where[name][piece]], preferred_element_type=F32)

    cacc[...] = coeff(yown[0], "me", 0)
    for piece in (2, 1, 3):
        cacc[...] += coeff(yown[piece], "me", piece)

    for copy in gram_sends:
        copy.wait_recv()
    total = gin[0]
    for w in range(1, 8):
        total = total + gin[w]
    part[...] = total
    z_sends = []
    for i in range(1, 8):
        w, device = z_peer(i)
        copy = remote(part, zin.at[z], zss.at[i], zrs.at[i], device)
        copy.start()
        z_sends.append(copy)
    zin[z] = total

    def sides(piece):
        gather_left[piece].wait_recv()
        cacc[...] += coeff(yr[piece], "right", piece)
        gather_right[piece].wait_recv()
        cacc[...] += coeff(yl[piece], "left", piece)

    forward = [None] * 4

    def relay(piece):
        h = piece % 2
        if piece < 2:
            forward[piece] = send(yr.at[piece], yopp.at[piece], fsl.at[h], frr.at[h], left)
        else:
            forward[piece] = send(yl.at[piece], yopp.at[piece], fsr.at[h], frl.at[h], right)

    sides(0)
    sides(2)

    for copy in z_sends:
        copy.wait_recv()
    total = zin[0]
    for w in range(1, 8):
        total = total + zin[w]
    part_x[...] = total
    x_sends = []
    for i in (2, 1, 3):
        copy = remote(part_x, xin.at[me], xss.at[i], xrs.at[i], ids(node, lax.rem(me + i, 4)))
        copy.start()
        x_sends.append(copy)
    xin[me] = total

    relay(0)
    relay(2)
    sides(1)
    relay(1)
    sides(3)
    relay(3)

    for copy in x_sends:
        copy.wait_recv()
    total = xin[0]
    for w in range(1, 4):
        total = total + xin[w]
    gfull[pl.ds(v * 3, 3)] = total
    share_sends = []
    for i in range(1, 8):
        w, device = v_peer(i)
        copy = remote(gfull.at[pl.ds(v * 3, 3)], gfull.at[pl.ds(v * 3, 3)], ass.at[i], ars.at[i], device)
        copy.start()
        share_sends.append(copy)

    for piece in (0, 2, 1, 3):
        forward[piece].wait_recv()
        cacc[...] += coeff(yopp[piece], "opp", piece)
    top = cacc[0:128, :].T
    rest = cacc[128:160, :].T
    for w in range(8):
        for zl in range(2):
            start = (zl * 8 + w) * 32
            cp[w, zl * 32:(zl + 1) * 32, :] = top[start:start + 32, :]
            for h in range(2):
                g = zl * 2 + h
                cp[w, 64:80, g * 32:(g + 1) * 32] = rest[start + h * 16:start + h * 16 + 16, :]
    coeff_sends = []
    for i in (4, 3, 5, 2, 6, 1, 7):
        w, device = v_peer(i)
        copy = remote(cp.at[w], cin.at[v], css.at[i], crs.at[i], device)
        copy.start()
        coeff_sends.append(copy)
    cin[v] = cp[v]

    for copy in share_sends:
        copy.wait_recv()

    lower = gfull[0:20].reshape(R, 128) * scale
    m_ref[:, 0:128] = lower
    m_ref[0:128, 128:160] = lower[128:160, :].T
    m_ref[128:160, 128:160] = gfull[20:24].reshape(32, 128)[:, 0:32] * scale
    lane = lax.broadcasted_iota(jnp.int32, (1, R), 1)
    lanes = lax.broadcasted_iota(jnp.int32, (PANEL, R), 1)
    row_id = lax.broadcasted_iota(jnp.int32, (PANEL, R), 0)

    whole = m_ref[...]
    square = lax.broadcasted_iota(jnp.int32, (R, R), 0) == lax.broadcasted_iota(jnp.int32, (R, R), 1)
    diagonal = jnp.where(square, whole, 0.0)
    fit = lax.rsqrt(jnp.sum(diagonal, axis=0, keepdims=True))
    m_ref[...] = whole * lax.rsqrt(jnp.sum(diagonal, axis=1, keepdims=True)) * fit

    def panel(p):
        base = p * PANEL
        block = m_ref[base:base + PANEL, :]
        dinv = jnp.zeros((PANEL, R), F32)
        for t in range(0, PANEL, 2):
            k = base + t
            c0 = jnp.broadcast_to(block[:, k:k + 1], (PANEL, R))
            c1 = jnp.broadcast_to(block[:, k + 1:k + 2], (PANEL, R))
            a, b, c = c0[t:t + 1, :], c0[t + 1:t + 2, :], c1[t + 1:t + 2, :]
            over = 1.0 / (a * c - b * b)
            first = 1.0 / a
            dinv = jnp.where(row_id == t, first, jnp.where(row_id == t + 1, a * over, dinv))
            row0, row1 = block[t:t + 1, :], block[t + 1:t + 2, :]
            row0 = jnp.where(lane == k, row0 + 1.0, row0)
            row1 = jnp.where(lane == k + 1, row1 + 1.0, row1)
            low = row_id > t + 1
            block = (block - jnp.where(low, c0, 0.0) * ((c * row0 - b * row1) * over)
                     - jnp.where(low, c1, 0.0) * ((a * row1 - b * row0) * over)
                     - jnp.where(row_id == t + 1, b * first * row0, 0.0))
        rows = row_id + base
        unit = jnp.where(lanes < rows, block, jnp.where(lanes == rows, 1.0, 0.0))
        inv_ref[base:base + PANEL, :] = unit * jnp.sqrt(dinv) * fit
        if base + PANEL < R:
            inside = (lanes >= base) & (lanes < base + PANEL)
            rest = jnp.where(inside, unit, block)
            update = lax.dot_general(block * dinv, rest, (((0,), (0,)), ((), ())),
                                     precision=HIGH, preferred_element_type=F32)
            below = slice(base + PANEL, R)
            keep = jnp.where((lane >= base) & (lane < base + PANEL), 0.0, m_ref[below, :])
            m_ref[below, :] = keep - update[below, :]

    panel(0)

    panel(1)

    for copy in coeff_sends:
        copy.wait_recv()
    small = cin[0]
    for w in range(1, 8):
        small = small + cin[w]
    for t in range(8):
        g, h = t // 2, t % 2
        csum[t, :, 0:128] = small[t * 8:t * 8 + 8, :]
        csum[t, :, 128:160] = small[64 + h * 8:72 + h * 8, g * 32:(g + 1) * 32]

    def mine(t):
        return jnp.logical_and(2 * me + t // 4 == z, me == t % 4)

    for t in range(8):
        @pl.when(jnp.logical_not(mine(t)))
        def _():
            remote(csum.at[t], cz.at[z], dss.at[t], drs.at[z], ids((2 * me + t // 4) * 8 + v, t % 4)).start()

        @pl.when(mine(t))
        def _():
            cz[z] = csum[t]

    panel(2)
    panel(3)
    inv = inv_ref[...]
    core_ref[...] = jnp.dot(inv, y_ref[...], precision=HIGH, preferred_element_type=F32)

    for pair in to_left + to_right:
        pair[0].wait_send()
        pair[1].wait_send()
    for copy in gather_left + gather_right + forward + coeff_sends + z_sends + gram_sends + x_sends + share_sends:
        copy.wait_send()
    for zs in range(8):
        @pl.when(jnp.logical_or(zs != z, source_x != me))
        def _():
            remote(csum.at[0], cz.at[zs], dss.at[0], drs.at[zs], ids(node, me)).wait_recv()
    out = cz[0]
    for w in range(1, 8):
        out = out + cz[w]
    next_ref[...] = lax.dot_general(out * scale, inv, NT, precision=HIGH, preferred_element_type=F32)

    for t in range(8):
        @pl.when(jnp.logical_not(mine(t)))
        def _():
            remote(csum.at[t], cz.at[0], dss.at[t], drs.at[0], ids(node, me)).wait_send()


def body(snapshots, sketch_matrix):
    node_total = snapshots.shape[0] * lax.axis_size("node")
    vmem = pl.BlockSpec(memory_space=pltpu.VMEM)
    dma = pltpu.SemaphoreType.DMA
    shape = jax.ShapeDtypeStruct
    scratch = pltpu.VMEM
    core, nxt = pl.pallas_call(
        functools.partial(fused_kernel, 1.0 / node_total),
        out_shape=(shape((R, 2048), F32), shape((8, R), F32)),
        in_specs=[pl.BlockSpec(memory_space=pltpu.HBM), vmem],
        out_specs=(vmem, vmem),
        scratch_shapes=[
            scratch((16, PC, PC), BF16),
            scratch((6, R, PC), BF16), scratch((6, R, PC), BF16),
            scratch((6, R, PC), BF16), scratch((6, R, PC), BF16),
            scratch((6, 8, 128), F32), scratch((6, 8, 128), F32),
            scratch((6, 8, 128), F32), scratch((6, 8, 128), F32),
            scratch((4, R, PC), F32), scratch((R, 2048), F32),
            scratch((4, R, PC), BF16), scratch((4, R, PC), BF16),
            scratch((4, R, PC), BF16), scratch((4, R, PC), BF16),
            scratch((R, PC), F32), scratch((R, R), F32),
            scratch((24, 8, 128), F32), scratch((8, 3, 8, 128), F32), scratch((3, 8, 128), F32),
            scratch((8, 3, 8, 128), F32), scratch((3, 8, 128), F32), scratch((4, 3, 8, 128), F32),
            scratch((24, 8, 128), F32),
            scratch((8, 80, 128), F32), scratch((8, 80, 128), F32),
            scratch((8, 8, R), F32), scratch((8, 8, R), F32),
            scratch((R, R), F32), scratch((R, R), F32),
            dma((16,)), dma((6,)), dma((6,)), dma((6,)), dma((6,)),
            dma((6,)), dma((6,)), dma((6,)), dma((6,)),
            dma((4,)), dma((4,)), dma((4,)), dma((4,)),
            dma((2,)), dma((2,)), dma((2,)), dma((2,)),
            pltpu.SemaphoreType.REGULAR((5,)),
            dma((8,)), dma((8,)), dma((8,)), dma((8,)), dma((4,)), dma((4,)), dma((8,)), dma((8,)),
            dma((8,)), dma((8,)), dma((8,)), dma((8,)),
        ],
        compiler_params=pltpu.CompilerParams(collective_id=0, has_side_effects=True, vmem_limit_bytes=50 << 20),
    )(snapshots, sketch_matrix.T)
    return core.T, nxt.T


def solution(mesh):
    placed = (P("node", "samp"), P("samp", None))
    return jax.shard_map(
        body,
        mesh=mesh,
        in_specs=placed,
        out_specs=(P(("node", "samp"), None), P("node", "samp")),
        check_vma=False,
    )
```
